128 devices in a mesh: group: 8 (over x, core), sub: 16 (over z, y).
Axes of the slice: x: 4, y: 4, z: 4, core: 2. Of those that a mesh axis runs over, the one named last changes fastest.
Arguments:
- schur: bfloat16 [8, 16, 1024, 1024], P('group', 'sub'), as said below
- local_inverse: bfloat16 [8, 16, 1024, 1024], P('group', 'sub'), as said below
- rhs_parts: bfloat16 [8, 16, 1024, 128], P('group', 'sub'), may hold values from -6 to 6
- basis: bfloat16 [8, 16, 32, 1024], P('group', 'sub'), may hold values from -0.1875 to 0.1875
- coarse_map: int32 [8, 16, 32], P('group', 'sub'), may hold values from 0 to 1023
- coarse_inverse: bfloat16 [8, 1024, 1024], P('group', 'sub'), as said below
- shared_rows: int32 [8, 16, 2, 4, 256], P('group', 'sub'), may hold values from 0 to 1023, as said below
- shared_counts: int32 [8, 16, 4], P('group', 'sub'), may hold values from 0 to 256, as said below
Outputs:
- solution: float32 [8, 16, 1024, 128], P('group', 'sub')
- residual: float32 [8, 16, 1024, 128], P('group', 'sub')
The draws below stay inside these ranges and needn't reach their ends.
Inputs may be any that keep to these rules, and one draw needn't show every extreme that they name: `schur`: each subdomain matrix is symmetric positive definite. `local_inverse`: each subdomain matrix is symmetric positive definite. `coarse_inverse`: each group's matrix is symmetric positive definite. `shared_rows`: own rows of direction d lie in rows d * 256 to (d + 1) * 256 - 1 and are distinct within a list; the own rows of direction 0 of (g, s) are the partner rows of direction 1 of (g, s + 1) and the reverse, likewise directions 2 and 3 between (g, s) and (g + 1, s); entries past the count are rows of the same block. `shared_counts`: the count of direction 0 of (g, s) equals the count of direction 1 of (g, s + 1), that of direction 2 of (g, s) the count of direction 3 of (g + 1, s); counts are 0 where no neighbour exists; some count equals 256.
All inputs are finite; a program needn't handle non-finite values.
Results may differ from the reference program's by a relative error of at most 0.014.
Values may be sent and summed in bfloat16 or wider, within the bound.
A program may use at most 64 MiB of HBM per device.

```python
import math
import jax
import jax.numpy as jnp
from jax import lax

NL = 1024
NRHS = 128
NC = 32
NC0 = 1024
ITERS = 3
CAP = 256
SUBS = 16
GROUPS = 8


def spd_stack(key, total_count, matrix_order):

    def single(position):
        sub_key = jax.random.fold_in(key, position)
        noise_key, diag_key = jax.random.split(sub_key)
        noise_draw = jax.random.normal(noise_key, (matrix_order, matrix_order), jnp.float32)
        diagonal = jax.random.uniform(diag_key, (matrix_order,), jnp.float32, 1.2, 3.0)
        symmetric = (noise_draw + noise_draw.T) * (0.45 / math.sqrt(2.0 * matrix_order))
        return (symmetric + jnp.diag(diagonal)).astype(jnp.bfloat16)
    return lax.map(single, jnp.arange(total_count))


def draw_schur(key, part):
    return spd_stack(jax.random.fold_in(key, 11), GROUPS * SUBS, NL).reshape(GROUPS, SUBS, NL, NL)


def draw_local_inverse(key, part):
    return spd_stack(jax.random.fold_in(key, 23), GROUPS * SUBS, NL).reshape(GROUPS, SUBS, NL, NL)


def draw_coarse_inverse(key, part):
    return spd_stack(jax.random.fold_in(key, 37), GROUPS, NC0)


def interface_plan(key):
    zone_rows = NL // 4
    keys = jax.random.split(jax.random.fold_in(key, 41), 6)
    base = jnp.broadcast_to(jnp.arange(zone_rows, dtype=jnp.int32), (GROUPS, SUBS, zone_rows))
    chain_low = jax.random.permutation(keys[0], base, axis=2, independent=True)
    chain_high = jax.random.permutation(keys[1], base, axis=2, independent=True)
    group_low = jax.random.permutation(keys[2], base, axis=2, independent=True)
    group_high = jax.random.permutation(keys[3], base, axis=2, independent=True)
    sub_pos = jnp.arange(SUBS, dtype=jnp.int32)[None, :]
    group_pos = jnp.arange(GROUPS, dtype=jnp.int32)[:, None]
    chain_count = jax.random.randint(keys[4], (GROUPS, SUBS), zone_rows // 4, zone_rows + 1, dtype=jnp.int32)
    chain_count = chain_count.at[0, 0].set(zone_rows)
    chain_count = jnp.where(sub_pos < SUBS - 1, chain_count, 0)
    group_count = jax.random.randint(keys[5], (GROUPS, SUBS), zone_rows // 4, zone_rows + 1, dtype=jnp.int32)
    group_count = group_count.at[0, 0].set(zone_rows)
    group_count = jnp.where(group_pos < GROUPS - 1, group_count, 0)
    own = jnp.stack([chain_low, zone_rows + jnp.roll(chain_high, 1, axis=1), 2 * zone_rows + group_low, 3 * zone_rows + jnp.roll(group_high, 1, axis=0)], axis=2)
    partner = jnp.stack([zone_rows + chain_high, jnp.roll(chain_low, 1, axis=1), 3 * zone_rows + group_high, 2 * zone_rows + jnp.roll(group_low, 1, axis=0)], axis=2)
    rows_all = jnp.stack([own, partner], axis=2).astype(jnp.int32)
    counts_all = jnp.stack([chain_count, jnp.where(sub_pos > 0, jnp.roll(chain_count, 1, axis=1), 0), group_count, jnp.where(group_pos > 0, jnp.roll(group_count, 1, axis=0), 0)], axis=2).astype(jnp.int32)
    return (rows_all, counts_all)


def draw_shared_rows(key, part):
    return interface_plan(key)[0]


def draw_shared_counts(key, part):
    return interface_plan(key)[1]


def plant(values, stream_key, smallest, largest):
    spot = [jax.random.randint(jax.random.fold_in(stream_key, axis), (), 0, length) for axis, length in enumerate(values.shape)]
    main_axis = values.shape.index(max(values.shape))
    next_to = spot[:main_axis] + [(spot[main_axis] + 1) % values.shape[main_axis]] + spot[main_axis + 1:]
    return values.at[tuple(spot)].set(smallest).at[tuple(next_to)].set(largest)


def levels(key, extent, pieces, least, largest):
    gain, own = 1.0, jax.random.fold_in(key, 6)
    for dim, parts in pieces:
        draws = jnp.exp(jax.random.uniform(jax.random.fold_in(own, dim), (parts,), jnp.float32, least / len(pieces), largest / len(pieces)))
        gain = gain * jnp.repeat(draws, extent[dim] // parts).reshape([-1 if axis == dim else 1 for axis in range(len(extent))])
    return gain


def noise(rng, shape, deviation, most, cuts=(), kind=jnp.bfloat16):
    array = jax.random.normal(rng, shape, jnp.float32) * deviation
    if len(cuts) > 0:
        array = levels(rng, shape, cuts, -0.22, 0.18) * array
    return jnp.clip(array, min=-most, max=most).astype(kind)


def setup_inputs(seed: int = 0) -> dict:
    arg_keys = jax.random.split(jax.random.key(seed), 9)
    return {
        "schur": draw_schur(jax.random.fold_in(arg_keys[8], 71), 0),
        "local_inverse": draw_local_inverse(jax.random.fold_in(arg_keys[8], 71), 0),
        "rhs_parts": noise(arg_keys[2], (GROUPS, SUBS, NL, NRHS), 1.0, 6.0, ((0, 8), (1, 16))),
        "basis": noise(arg_keys[3], (GROUPS, SUBS, NC, NL), NL ** -0.5, 0.1875, ((0, 8), (1, 16))),
        "coarse_map": plant(jax.random.randint(arg_keys[4], (GROUPS, SUBS, NC), 0, NC0), jax.random.fold_in(arg_keys[4], 1), 0, NC0 - 1).astype(jnp.int32),
        "coarse_inverse": draw_coarse_inverse(jax.random.fold_in(arg_keys[8], 71), 0),
        "shared_rows": draw_shared_rows(jax.random.fold_in(arg_keys[8], 71), 0),
        "shared_counts": draw_shared_counts(jax.random.fold_in(arg_keys[8], 71), 0),
    }


def pick_rows(tables, indices):
    return jax.vmap(jax.vmap(lambda source_block, rows_at: source_block[rows_at]))(tables, indices)

def add_rows(bases, indices, additions):

    def single(base_block, rows_at, extra):
        return base_block.at[rows_at.reshape(-1)].add(extra.reshape(-1, base_block.shape[-1]))
    return jax.vmap(jax.vmap(single))(bases, indices, additions)

def count_rows(indices, live_mask):

    def single(rows_at, mask_rows):
        return jnp.ones((NL,), jnp.float32).at[rows_at.reshape(-1)].add(mask_rows.reshape(-1))
    return jax.vmap(jax.vmap(single))(indices, live_mask)

def assemble(blocks, own_rows, partner_rows, live_mask):
    blocks = blocks.astype(jnp.float32)
    zero_sub = jnp.zeros_like(blocks[:, :1])
    zero_group = jnp.zeros_like(blocks[:1])
    next_chain = jnp.concatenate([blocks[:, 1:], zero_sub], axis=1)
    prev_chain = jnp.concatenate([zero_sub, blocks[:, :-1]], axis=1)
    next_group = jnp.concatenate([blocks[1:], zero_group], axis=0)
    prev_group = jnp.concatenate([zero_group, blocks[:-1]], axis=0)
    received = jnp.stack([pick_rows(next_chain, partner_rows[:, :, 0]), pick_rows(prev_chain, partner_rows[:, :, 1]), pick_rows(next_group, partner_rows[:, :, 2]), pick_rows(prev_group, partner_rows[:, :, 3])], axis=2)
    values = received * live_mask[..., None]
    return add_rows(blocks, own_rows, values)

def batch_apply(matrices, vectors, transpose_left):
    lead = matrices.shape[:2]
    flat_mats = matrices.reshape((-1,) + matrices.shape[2:])
    flat_vecs = vectors.reshape((-1,) + vectors.shape[2:])

    def single(pair):
        left = pair[0].T if transpose_left else pair[0]
        return jnp.dot(left.astype(jnp.float32), pair[1].astype(jnp.float32), preferred_element_type=jnp.float32)
    result = lax.map(single, (flat_mats, flat_vecs))
    return result.reshape(lead + result.shape[1:])

def gram_matrix(left, right, weight):
    return jnp.einsum('gsir,gsic->rc', left * weight[..., None], right, precision=lax.Precision.HIGHEST)

def spd_solve(matrix, rhs_block):
    factor = jnp.linalg.cholesky(matrix)
    half = lax.linalg.triangular_solve(factor, rhs_block, left_side=True, lower=True)
    return lax.linalg.triangular_solve(factor, half, left_side=True, lower=True, transpose_a=True)

def contract(blocks, mixing):
    return jnp.einsum('gsir,rc->gsic', blocks, mixing, precision=lax.Precision.HIGHEST)

def reference(schur, local_inverse, rhs_parts, basis, coarse_map, coarse_inverse, shared_rows, shared_counts):
    live_mask = (jnp.arange(CAP, dtype=jnp.int32) < shared_counts[..., None]).astype(jnp.float32)
    own_rows = shared_rows[:, :, 0]
    partner_rows = shared_rows[:, :, 1]
    weight = 1.0 / count_rows(own_rows, live_mask)

    def precondition(resid):
        scaled = (weight[..., None] * resid).astype(jnp.bfloat16)
        local_part = batch_apply(local_inverse, scaled, False)
        coarse_local = batch_apply(basis, scaled, False)

        def group_sum(mapping, terms):
            return jnp.zeros((NC0, NRHS), jnp.float32).at[mapping.reshape(-1)].add(terms.reshape(-1, NRHS))
        coarse_residual = jax.vmap(group_sum)(coarse_map, coarse_local)
        coarse_rounded = coarse_residual.astype(jnp.bfloat16)
        coarse_values = lax.map(lambda pair: jnp.dot(pair[0].astype(jnp.float32), pair[1].astype(jnp.float32), preferred_element_type=jnp.float32), (coarse_inverse, coarse_rounded)).astype(jnp.bfloat16)
        picked = jax.vmap(lambda values_group, mapping: values_group[mapping])(coarse_values, coarse_map)
        coarse_part = batch_apply(basis, picked, True)
        smoothed = weight[..., None] * (local_part + coarse_part)
        return assemble(smoothed, own_rows, partner_rows, live_mask)
    residual = assemble(rhs_parts.astype(jnp.float32), own_rows, partner_rows, live_mask)
    solution = jnp.zeros_like(residual)
    precond = precondition(residual)
    direction = precond
    inner = gram_matrix(precond, residual, weight)
    for iteration in range(ITERS):
        local_image = batch_apply(schur, direction.astype(jnp.bfloat16), False)
        image = assemble(local_image, own_rows, partner_rows, live_mask)
        curvature = gram_matrix(direction, image, weight)
        step_size = spd_solve(curvature, inner)
        solution = solution + contract(direction, step_size)
        residual = residual - contract(image, step_size)
        if iteration + 1 < ITERS:
            precond = precondition(residual)
            inner_next = gram_matrix(precond, residual, weight)
            conjugacy = spd_solve(inner, inner_next)
            direction = precond + contract(direction, conjugacy)
            inner = inner_next
    return (solution, residual)
```

```python
import functools

import jax
import jax.numpy as jnp
from jax import lax
from jax.experimental import pallas as pl
from jax.experimental.pallas import tpu as pltpu
from jax.sharding import PartitionSpec as P

BF = jnp.bfloat16
F32 = jnp.float32
MESH = pl.DeviceIdType.MESH
N_GROUP = 8
N_SUB = 16
NL = 1024
ZONE = 256
NR = 128
NC = 32
NC_ALL = NC * N_SUB
OWN_ROWS = 64
AR_ROWS = (256, 256, 128, 128)


def split(x):
    hi = x.astype(BF)
    lo = (x - hi.astype(F32)).astype(BF)
    return jnp.concatenate([hi, lo], axis=-1)


def fold(y):
    return y[:, :NR] + y[:, NR:]


def dot(a, b, dims=((1,), (0,))):
    return lax.dot_general(a, b, (dims, ((), ())), preferred_element_type=F32)


def small(a, b):
    return jnp.dot(a, b, precision=lax.Precision.HIGHEST, preferred_element_type=F32)


def gram(left, right):
    full = dot(left, right, ((0,), (0,)))
    half = full[:NR] + full[NR:]
    return half[:, :NR] + half[:, NR:]


def sym(a):
    return 0.5 * (a + a.T)


def combine(blocks, mixing):
    halves = split(mixing)
    return fold(dot(blocks, jnp.concatenate([halves, halves], axis=0)))


def invert_steps(mat, first, last):
    lane = lax.broadcasted_iota(jnp.int32, (NR, NR), 1)
    lane_row = lax.broadcasted_iota(jnp.int32, (1, NR), 1)
    sub = lax.broadcasted_iota(jnp.int32, (NR, NR), 0)

    def step(k, carry):
        a = mat[...]
        row = mat[pl.ds(k, 1), :]
        here = lane == k
        col = jnp.sum(jnp.where(here, a, 0.0), axis=1, keepdims=True)
        pivot = jnp.sum(jnp.where(lane_row == k, row, 0.0), axis=1, keepdims=True)
        scaled = jnp.where(lane_row == k, 1.0, row) / pivot
        new = jnp.where(here, 0.0, a) - col * scaled
        mat[...] = jnp.where(sub == k, scaled, new)
        return carry

    lax.fori_loop(first, last, step, 0)


def kernel(
    schur_h, linv_h, rhs, basis, cmap, cinv, rows, counts,
    x_out, r_out,
    schur, linv, perm, weight, mult, sent, got0, got, r0, xw, xz, loc, base,
    cl_mine, cl_all, map_mine, map_all, e_mine, e_all, coarse, mu, inv,
    ar_in, ar_r1, ar_p, ar_r2, ar_q, ar_out,
    load_sem, xs, xr, cs, cr, ms, mr, es, er, as1, ar1, as2, ar2, as3, ar3,
):
    g = lax.axis_index("group")
    s = lax.axis_index("sub")
    started = []

    def remote(src, dst, send_sem, recv_sem, target):
        copy = pltpu.make_async_remote_copy(
            src_ref=src, dst_ref=dst, send_sem=send_sem, recv_sem=recv_sem,
            device_id=target, device_id_type=MESH,
        )
        copy.start()
        started.append(copy)
        return copy

    load_l = pltpu.make_async_copy(linv_h, linv, load_sem.at[0])
    load_s = pltpu.make_async_copy(schur_h, schur, load_sem.at[1])
    load_l.start()
    load_s.start()

    barrier = pltpu.get_barrier_semaphore()
    mates = [(g, lax.rem(s + k, N_SUB)) for k in range(1, N_SUB)]
    peers = [(lax.rem(g + k, N_GROUP), s) for k in range(1, N_GROUP)]
    for target in mates + peers:
        pl.semaphore_signal(barrier, inc=1, device_id=target, device_id_type=MESH)

    map_mine[...] = jnp.zeros((8, NR), jnp.int32)
    map_mine[0:1, 0:NC] = cmap[...]
    tile = jnp.broadcast_to(map_mine[0:1, :], (8, NR))
    tile = pltpu.roll(tile, NC * lax.rem(s, 4), 1)
    at_row = lax.broadcasted_iota(jnp.int32, (8, NR), 0) == lax.div(s, 4)
    map_mine[...] = jnp.where(at_row, tile, 0)

    pl.semaphore_wait(barrier, len(mates) + len(peers))

    around = [
        (g, lax.rem(s + 1, N_SUB)),
        (g, lax.rem(s + N_SUB - 1, N_SUB)),
        (lax.rem(g + 1, N_GROUP), s),
        (lax.rem(g + N_GROUP - 1, N_GROUP), s),
    ]

    def send_zone(e, d, src, dst):
        return remote(src, dst.at[d ^ 1], xs.at[e, d], xr.at[e, d ^ 1], around[d])

    def zone(d):
        return pl.ds(ZONE * d, ZONE)

    copies0 = [send_zone(0, d, rhs.at[zone(d)], got0) for d in range(4)]
    map_copies = [
        remote(map_mine, map_all.at[k], ms.at[k], mr.at[k], mates[k - 1])
        for k in range(1, N_SUB)
    ]

    lane = lax.broadcasted_iota(jnp.int32, (1, ZONE), 1)
    at = lax.broadcasted_iota(jnp.int32, (ZONE, ZONE), 0)
    for d in range(4):
        mine = jnp.where(lane < counts[0, d], rows[0, d : d + 1, :] - ZONE * d, -1)
        theirs = rows[1, d : d + 1, :] - ZONE * (d ^ 1)
        place = jnp.where(at == mine, 1.0, 0.0)
        times = 1.0 + jnp.sum(place, axis=1, keepdims=True)
        mult[zone(d), :] = jnp.broadcast_to(times, (ZONE, NR))
        weight[zone(d), :] = jnp.broadcast_to(1.0 / times, (ZONE, NR))
        pick = jnp.where(at == theirs, 1.0, 0.0).astype(BF)
        perm[d] = dot(place.astype(BF), pick, ((1,), (1,))).astype(BF)

    for d in range(4):
        copies0[d ^ 1].wait_recv()
        block = rhs[zone(d), :].astype(F32) + dot(perm[d], got0[d])
        r0[zone(d), :] = block
        xw[0, zone(d), :] = split(weight[zone(d), :] * block)

    def coarse_send(k):
        local = fold(dot(basis[...], xw[k]))
        cl_mine[k] = local
        copies = [
            remote(cl_mine.at[k], cl_all.at[k, s], cs.at[k, i + 1], cr.at[k, i + 1], mates[i])
            for i in range(N_SUB - 1)
        ]
        cl_all[k, s] = local
        return copies

    def coarse_setup():
        for copy in map_copies:
            copy.wait_recv()
        total = map_mine[...]
        for k in range(1, N_SUB):
            total = total + map_all[k]
        at_all = lax.broadcasted_iota(jnp.int32, (NL, NR), 0)
        at_own = lax.broadcasted_iota(jnp.int32, (OWN_ROWS, NR), 0) + OWN_ROWS * s
        hot = jnp.concatenate(
            [jnp.where(at_all == total[i : i + 1, :], 1.0, 0.0).astype(BF) for i in range(4)], axis=1
        )
        hot_own = jnp.concatenate(
            [jnp.where(at_own == total[i : i + 1, :], 1.0, 0.0).astype(BF) for i in range(4)], axis=1
        )
        columns = dot(cinv[...], hot).astype(BF)
        entries = dot(hot_own, columns, ((0,), (0,))).astype(BF)
        e_mine[...] = entries.reshape(N_SUB, NC, NC_ALL)
        copies = [
            remote(
                e_mine.at[lax.rem(s + k, N_SUB)], e_all.at[s], es.at[k], er.at[k], mates[k - 1]
            )
            for k in range(1, N_SUB)
        ]
        e_all[s] = e_mine[s]
        return copies

    def local_apply(matrix, blocks, d):
        return fold(dot(matrix[zone(d), :], blocks))

    def precondition(k, e, during):
        copies = coarse_send(k)
        if k == 0:
            e_copies = coarse_setup()
            load_l.wait()
        blocks = xw[k]
        for d in range(4):
            loc[zone(d), :] = local_apply(linv, blocks, d)
        during()
        if k == 0:
            for copy in e_copies:
                copy.wait_recv()
            total = e_all[0].astype(F32)
            for i in range(1, N_SUB):
                total = total + e_all[i].astype(F32)
            coarse[...] = total.astype(BF)
        for copy in copies:
            copy.wait_recv()
        terms = split(cl_all[k].reshape(NC_ALL, NR))
        picked = split(fold(dot(coarse[...], terms)))
        sends = []
        for d in range(4):
            part = fold(dot(basis[:, zone(d)], picked, ((0,), (0,))))
            sent[e - 1, zone(d), :] = weight[zone(d), :] * (loc[zone(d), :] + part)
            sends.append(send_zone(e, d, sent.at[e - 1, zone(d)], got.at[e - 1]))
        return sends

    def operate(k, e):
        sends = []
        blocks = xz[k]
        for d in range(4):
            sent[e - 1, zone(d), :] = local_apply(schur, blocks, d)
            sends.append(send_zone(e, d, sent.at[e - 1, zone(d)], got.at[e - 1]))
        return sends

    def assembled(e, sends, d):
        sends[d ^ 1].wait_recv()
        return sent[e - 1, zone(d), :] + fold(dot(perm[d], split(got[e - 1, d])))

    def finish_z(k, e, sends):
        for d in range(4):
            xz[k, zone(d), :] = split(assembled(e, sends, d))

    def finish_q(k, e, sends):
        for d in range(4):
            xw[k + 1, zone(d), :] = split(weight[zone(d), :] * assembled(e, sends, d))

    def reduce_start(i):
        share = AR_ROWS[i] // N_GROUP
        copies = []
        for k in range(1, N_GROUP):
            src = ar_in[i].at[pl.ds(pl.multiple_of(share * peers[k - 1][0], 8), share)]
            copies.append(
                remote(src, ar_r1[i].at[g], as1.at[i, k], ar1.at[i, k], peers[k - 1])
            )
        ar_r1[i][g] = ar_in[i][pl.ds(pl.multiple_of(share * g, 8), share), :]
        return copies

    def reduce_middle(i, waits):
        for copy in waits:
            copy.wait_recv()
        total = ar_r1[i][0]
        for k in range(1, N_GROUP):
            total = total + ar_r1[i][k]
        ar_p[i][...] = total
        copies = [
            remote(ar_p[i], ar_r2[i].at[s], as2.at[i, k], ar2.at[i, k], mates[k - 1])
            for k in range(1, N_SUB)
        ]
        ar_r2[i][s] = total
        return copies

    def reduce_last(i, waits):
        share = AR_ROWS[i] // N_GROUP
        for copy in waits:
            copy.wait_recv()
        total = ar_r2[i][0]
        for k in range(1, N_SUB):
            total = total + ar_r2[i][k]
        ar_q[i][...] = total
        mine = pl.ds(pl.multiple_of(share * g, 8), share)
        copies = [
            remote(ar_q[i], ar_out[i].at[mine], as3.at[i, k], ar3.at[i, k], peers[k - 1])
            for k in range(1, N_GROUP)
        ]
        ar_out[i][mine, :] = total
        return copies

    def reduce_wait(waits):
        for copy in waits:
            copy.wait_recv()

    def nothing():
        pass

    state = {}

    sends = precondition(0, 1, nothing)
    finish_z(0, 1, sends)
    load_s.wait()
    sends = operate(0, 2)
    ar_in[0][0:NR, :] = gram(xz[0], xw[0])
    finish_q(0, 2, sends)
    ar_in[0][NR:, :] = gram(xz[0], xw[1])
    state["a"] = reduce_start(0)

    def during1():
        state["a"] = reduce_middle(0, state["a"])

    sends = precondition(1, 3, during1)
    state["a"] = reduce_last(0, state["a"])
    finish_z(1, 3, sends)
    sends = operate(1, 4)
    ar_in[1][0:NR, :] = gram(xz[1], xw[1])
    reduce_wait(state["a"])
    mu[0] = ar_out[0][0:NR, :]
    inv[0] = sym(ar_out[0][NR:, :])
    invert_steps(inv.at[0], 0, 32)
    finish_q(1, 4, sends)
    ar_in[1][NR:, :] = gram(xz[1], xw[2])
    state["b"] = reduce_start(1)

    def during2():
        invert_steps(inv.at[0], 32, 64)
        state["b"] = reduce_middle(1, state["b"])

    sends = precondition(2, 5, during2)
    invert_steps(inv.at[0], 64, 96)
    state["b"] = reduce_last(1, state["b"])
    finish_z(2, 5, sends)
    sends = operate(2, 6)
    ar_in[2][...] = gram(xz[2], xw[2])
    state["c"] = reduce_start(2)
    invert_steps(inv.at[0], 96, 128)
    reduce_wait(state["b"])
    finish_q(2, 6, sends)
    ar_in[3][...] = gram(xz[2], xw[3])
    state["d"] = reduce_start(3)
    state["c"] = reduce_middle(2, state["c"])
    m0 = mu[0]
    m2 = sym(ar_out[1][0:NR, :])
    m3 = sym(ar_out[1][NR:, :])
    inv1 = inv[0]
    t0 = small(inv1, m0)
    t2 = small(inv1, m2)
    t3 = small(inv1, m3)
    inv[1] = sym(m3 - small(m2, t2))
    h1 = sym(ar_out[0][NR:, :]) - small(m2, t0)
    state["d"] = reduce_middle(3, state["d"])
    state["c"] = reduce_last(2, state["c"])
    invert_steps(inv.at[1], 0, 64)
    state["d"] = reduce_last(3, state["d"])
    invert_steps(inv.at[1], 64, 128)
    reduce_wait(state["c"])
    m4 = sym(ar_out[2][...])
    inv2 = inv[1]
    s23 = m4 - small(m2, t3)
    y = small(inv2, s23)
    u1 = small(inv2, h1)
    h2 = m2 - small(m3, t0) - lax.dot_general(
        s23, u1, (((0,), (0,)), ((), ())), precision=lax.Precision.HIGHEST, preferred_element_type=F32
    )
    part = small(m3, t3) + lax.dot_general(
        s23, y, (((0,), (0,)), ((), ())), precision=lax.Precision.HIGHEST, preferred_element_type=F32
    )
    a0 = t0 - small(t2, u1)
    d0 = small(t2, y) - t3
    x_out[...] = combine(xz[0], a0) + combine(xz[1], u1)
    xd = xz[2]
    base[0] = split(
        xd[:, :NR].astype(F32) + xd[:, NR:].astype(F32) - combine(xz[1], y) + combine(xz[0], d0)
    )
    r_out[...] = r0[...] - mult[...] * (combine(xw[1], a0) + combine(xw[2], u1))
    qd = xw[3]
    base[1] = split(
        qd[:, :NR].astype(F32) + qd[:, NR:].astype(F32) - combine(xw[2], y) + combine(xw[1], d0)
    )
    reduce_wait(state["d"])
    inv[2] = sym(ar_out[3][...] - part)
    invert_steps(inv.at[2], 0, 128)
    c2 = small(inv[2], h2)
    x_out[...] = x_out[...] + combine(base[0], c2)
    r_out[...] = r_out[...] - mult[...] * combine(base[1], c2)
    for copy in started:
        copy.wait_send()


def shards(
    schur, local_inverse, rhs_parts, basis, coarse_map, coarse_inverse, shared_rows, shared_counts
):
    vmem = pl.BlockSpec(memory_space=pltpu.VMEM)
    anywhere = pl.BlockSpec(memory_space=pl.ANY)
    dma = pltpu.SemaphoreType.DMA
    ar_shapes = [r // N_GROUP for r in AR_ROWS]
    scratch = [
        pltpu.VMEM((NL, NL), BF),
        pltpu.VMEM((NL, NL), BF),
        pltpu.VMEM((4, ZONE, ZONE), BF),
        pltpu.VMEM((NL, NR), F32),
        pltpu.VMEM((NL, NR), F32),
        pltpu.VMEM((6, NL, NR), F32),
        pltpu.VMEM((4, ZONE, NR), BF),
        pltpu.VMEM((6, 4, ZONE, NR), F32),
        pltpu.VMEM((NL, NR), F32),
        pltpu.VMEM((4, NL, 2 * NR), BF),
        pltpu.VMEM((3, NL, 2 * NR), BF),
        pltpu.VMEM((NL, NR), F32),
        pltpu.VMEM((2, NL, 2 * NR), BF),
        pltpu.VMEM((3, NC, NR), F32),
        pltpu.VMEM((3, N_SUB, NC, NR), F32),
        pltpu.VMEM((8, NR), jnp.int32),
        pltpu.VMEM((N_SUB, 8, NR), jnp.int32),
        pltpu.VMEM((N_SUB, NC, NC_ALL), BF),
        pltpu.VMEM((N_SUB, NC, NC_ALL), BF),
        pltpu.VMEM((NC, NC_ALL), BF),
        pltpu.VMEM((1, NR, NR), F32),
        pltpu.VMEM((3, NR, NR), F32),
        [pltpu.VMEM((r, NR), F32) for r in AR_ROWS],
        [pltpu.VMEM((N_GROUP, r, NR), F32) for r in ar_shapes],
        [pltpu.VMEM((r, NR), F32) for r in ar_shapes],
        [pltpu.VMEM((N_SUB, r, NR), F32) for r in ar_shapes],
        [pltpu.VMEM((r, NR), F32) for r in ar_shapes],
        [pltpu.VMEM((r, NR), F32) for r in AR_ROWS],
        dma((2,)),
        dma((7, 4)),
        dma((7, 4)),
        dma((3, N_SUB)),
        dma((3, N_SUB)),
        dma((N_SUB,)),
        dma((N_SUB,)),
        dma((N_SUB,)),
        dma((N_SUB,)),
        dma((4, N_GROUP)),
        dma((4, N_GROUP)),
        dma((4, N_SUB)),
        dma((4, N_SUB)),
        dma((4, N_GROUP)),
        dma((4, N_GROUP)),
    ]
    out = jax.ShapeDtypeStruct((NL, NR), F32)
    x, r = pl.pallas_call(
        kernel,
        out_shape=(out, out),
        in_specs=[anywhere, anywhere, vmem, vmem, vmem, vmem, vmem,
                  pl.BlockSpec(memory_space=pltpu.SMEM)],
        out_specs=(vmem, vmem),
        scratch_shapes=scratch,
        compiler_params=pltpu.CompilerParams(
            collective_id=0, has_side_effects=True, vmem_limit_bytes=48 * 1024 * 1024
        ),
        name="block_cg",
    )(
        schur[0, 0], local_inverse[0, 0], rhs_parts[0, 0], basis[0, 0], coarse_map[0],
        coarse_inverse[0], shared_rows[0, 0], shared_counts[0],
    )
    return x[None, None], r[None, None]


def solution(mesh):
    placed = (
        P("group", "sub", None, None),
        P("group", "sub", None, None),
        P("group", "sub", None, None),
        P("group", "sub", None, None),
        P("group", "sub", None),
        P("group", "sub", None),
        P("group", "sub", None, None, None),
        P("group", "sub", None),
    )
    return jax.shard_map(
        shards,
        mesh=mesh,
        in_specs=placed,
        out_specs=(P("group", "sub", None, None), P("group", "sub", None, None)),
        check_vma=False,
    )
```

```python
import functools

import jax
import jax.numpy as jnp
from jax import lax
from jax.experimental import pallas as pl
from jax.experimental.pallas import tpu as pltpu
from jax.sharding import PartitionSpec as P

BF = jnp.bfloat16
F32 = jnp.float32
MESH = pl.DeviceIdType.MESH
N_GROUP = 8
N_SUB = 16
NL = 1024
ZONE = 256
NR = 128
NC = 32
NC_ALL = NC * N_SUB
OWN_ROWS = 64
AR_ROWS = (256, 256, 128, 128)


def split(x):
    hi = x.astype(BF)
    lo = (x - hi.astype(F32)).astype(BF)
    return jnp.concatenate([hi, lo], axis=-1)


def fold(y):
    return y[:, :NR] + y[:, NR:]


def dot(a, b, dims=((1,), (0,))):
    return lax.dot_general(a, b, (dims, ((), ())), preferred_element_type=F32)


def small(a, b):
    return jnp.dot(a, b, precision=lax.Precision.HIGHEST, preferred_element_type=F32)


def gram(left, right):
    full = dot(left, right, ((0,), (0,)))
    half = full[:NR] + full[NR:]
    return half[:, :NR] + half[:, NR:]


def sym(a):
    return 0.5 * (a + a.T)


def combine(blocks, mixing):
    halves = split(mixing)
    return fold(dot(blocks, jnp.concatenate([halves, halves], axis=0)))


def invert_steps(mat, first, last):
    lane = lax.broadcasted_iota(jnp.int32, (NR, NR), 1)
    sub = lax.broadcasted_iota(jnp.int32, (NR, NR), 0)
    lane8 = lax.broadcasted_iota(jnp.int32, (8, NR), 1)

    def column(a, lanes, j):
        return jnp.broadcast_to(
            jnp.sum(jnp.where(lanes == j, a, 0.0), axis=1, keepdims=True), a.shape
        )

    def step(i, carry):
        k = 4 * i
        a = mat[...]
        r = [jnp.broadcast_to(mat[pl.ds(k + j, 1), :], (8, NR)) for j in range(4)]
        c = [column(a, lane, k + j) for j in range(4)]
        d = [[column(r[m], lane8, k + j) for j in range(4)] for m in range(4)]
        inside = (lane8 >= k) & (lane8 < k + 4)
        q = [jnp.where(lane8 == k + j, 1.0, jnp.where(inside, 0.0, r[j])) for j in range(4)]
        i0 = 1.0 / (d[0][0] * d[1][1] - d[0][1] * d[1][0])

        def lead(x0, x1):
            return (d[1][1] * x0 - d[0][1] * x1) * i0, (d[0][0] * x1 - d[1][0] * x0) * i0

        e02, e12 = lead(d[0][2], d[1][2])
        e03, e13 = lead(d[0][3], d[1][3])
        f0, f1 = lead(q[0], q[1])
        s22 = d[2][2] - d[2][0] * e02 - d[2][1] * e12
        s23 = d[2][3] - d[2][0] * e03 - d[2][1] * e13
        s32 = d[3][2] - d[3][0] * e02 - d[3][1] * e12
        s33 = d[3][3] - d[3][0] * e03 - d[3][1] * e13
        g2 = q[2] - d[2][0] * f0 - d[2][1] * f1
        g3 = q[3] - d[3][0] * f0 - d[3][1] * f1
        i1 = 1.0 / (s22 * s33 - s23 * s32)
        w2 = (s33 * g2 - s23 * g3) * i1
        w3 = (s22 * g3 - s32 * g2) * i1
        w = [f0 - e02 * w2 - e03 * w3, f1 - e12 * w2 - e13 * w3, w2, w3]
        w = [x[0:1] for x in w]
        new = jnp.where((lane >= k) & (lane < k + 4), 0.0, a)
        new = new - (c[0] * w[0] + c[1] * w[1]) - (c[2] * w[2] + c[3] * w[3])
        for j in range(4):
            new = jnp.where(sub == k + j, w[j], new)
        mat[...] = new
        return carry

    lax.fori_loop(first // 4, last // 4, step, 0)


def kernel(
    schur_h, linv_h, rhs_h, basis_h, cmap_h, cinv_h, rows_h, counts_h,
    x_out, r_out,
    schur, linv, rhs, basis, cmap, cinv, rows, counts, perm, weight, mult, sent, got0, got, r0, xw, xz, loc, base,
    cl_mine, cl_all, map_mine, map_all, hot, e_mine, e_all, coarse, mu, inv,
    ar_in, ar_r1, ar_p, ar_r2, ar_q, ar_out,
    load_sem, xs, xr, cs, cr, ms, mr, es, er, as1, ar1, as2, ar2, as3, ar3, as4, ar4,
):
    g = lax.axis_index("group")
    s = lax.axis_index("sub")
    started = []

    def remote(src, dst, send_sem, recv_sem, target):
        copy = pltpu.make_async_remote_copy(
            src_ref=src, dst_ref=dst, send_sem=send_sem, recv_sem=recv_sem,
            device_id=target, device_id_type=MESH,
        )
        copy.start()
        started.append(copy)
        return copy

    pairs = (
        (cmap_h, cmap), (rhs_h, rhs), (rows_h, rows), (counts_h, counts),
        (basis_h, basis), (cinv_h, cinv), (linv_h, linv), (schur_h, schur),
    )
    loads = [pltpu.make_async_copy(a, b, load_sem.at[i]) for i, (a, b) in enumerate(pairs)]
    for load in loads:
        load.start()
    load_l, load_s = loads[6:]

    barrier = pltpu.get_barrier_semaphore()
    mates = [(g, lax.rem(s + k, N_SUB)) for k in range(1, N_SUB)]
    peers = [(lax.rem(g + k, N_GROUP), s) for k in range(1, N_GROUP)]
    y, z = lax.rem(s, 4), lax.div(s, 4)
    mates_y = [(g, 4 * z + lax.rem(y + k, 4)) for k in range(1, 4)]
    mates_z = [(g, 4 * lax.rem(z + k, 4) + y) for k in range(1, 4)]
    for target in mates + peers:
        pl.semaphore_signal(barrier, inc=1, device_id=target, device_id_type=MESH)

    map_mine[...] = jnp.zeros((8, NR), jnp.int32)
    loads[0].wait()
    map_mine[0:1, 0:NC] = cmap[...]
    tile = jnp.broadcast_to(map_mine[0:1, :], (8, NR))
    tile = pltpu.roll(tile, NC * lax.rem(s, 4), 1)
    at_row = lax.broadcasted_iota(jnp.int32, (8, NR), 0) == lax.div(s, 4)
    map_mine[...] = jnp.where(at_row, tile, 0)

    for load in loads[1:6]:
        load.wait()
    pl.semaphore_wait(barrier, len(mates) + len(peers))

    around = [
        (g, lax.rem(s + 1, N_SUB)),
        (g, lax.rem(s + N_SUB - 1, N_SUB)),
        (lax.rem(g + 1, N_GROUP), s),
        (lax.rem(g + N_GROUP - 1, N_GROUP), s),
    ]

    def send_zone(e, d, src, dst):
        return remote(src, dst.at[d ^ 1], xs.at[e, d], xr.at[e, d ^ 1], around[d])

    def zone(d):
        return pl.ds(ZONE * d, ZONE)

    copies0 = [send_zone(0, d, rhs.at[zone(d)], got0) for d in range(4)]
    map_copies = [
        remote(map_mine, map_all.at[k], ms.at[k], mr.at[k], mates[k - 1])
        for k in range(1, N_SUB)
    ]

    lane = lax.broadcasted_iota(jnp.int32, (1, ZONE), 1)
    at = lax.broadcasted_iota(jnp.int32, (ZONE, ZONE), 0)
    for d in range(4):
        mine = jnp.where(lane < counts[0:1, d : d + 1], rows[0, d : d + 1, :] - ZONE * d, -1)
        theirs = rows[1, d : d + 1, :] - ZONE * (d ^ 1)
        place = jnp.where(at == mine, 1.0, 0.0)
        times = 1.0 + jnp.sum(place, axis=1, keepdims=True)
        mult[zone(d), :] = jnp.broadcast_to(times, (ZONE, NR))
        weight[zone(d), :] = jnp.broadcast_to(1.0 / times, (ZONE, NR))
        pick = jnp.where(at == theirs, 1.0, 0.0).astype(BF)
        perm[d] = dot(place.astype(BF), pick, ((1,), (1,))).astype(BF)

    for d in (2, 3, 0, 1):
        copies0[d ^ 1].wait_recv()
        block = rhs[zone(d), :].astype(F32) + dot(perm[d], got0[d])
        r0[zone(d), :] = block
        xw[0, zone(d), :] = split(weight[zone(d), :] * block)

    def coarse_send(k):
        local = fold(dot(basis[...], xw[k]))
        cl_mine[k] = local
        copies = [
            remote(cl_mine.at[k], cl_all.at[k, s], cs.at[k, i + 1], cr.at[k, i + 1], mates[i])
            for i in range(N_SUB - 1)
        ]
        cl_all[k, s] = local
        return copies

    def coarse_setup():
        for copy in map_copies:
            copy.wait_recv()
        total = map_mine[...]
        for k in range(1, N_SUB):
            total = total + map_all[k]
        at_all = lax.broadcasted_iota(jnp.int32, (NL, NR), 0)
        for i in range(4):
            hot[:, NR * i : NR * (i + 1)] = jnp.where(
                at_all == total[i : i + 1, :], 1.0, 0.0
            ).astype(BF)
        picks = dot(cinv[...], hot[...]).T
        picks = jnp.concatenate([picks, picks], axis=1)
        half = lax.broadcasted_iota(jnp.int32, (NC_ALL, NR), 1) // OWN_ROWS
        picks = jnp.where(half == lax.rem(s, 2), picks, 0.0).astype(BF)
        e_mine[...] = picks.reshape(N_SUB, NC, NR)
        copies = [
            remote(
                e_mine.at[lax.rem(s + k, N_SUB)], e_all.at[s], es.at[k], er.at[k], mates[k - 1]
            )
            for k in range(1, N_SUB)
        ]
        e_all[s] = e_mine[s]
        return copies

    def coarse_finish(copies):
        for copy in copies:
            copy.wait_recv()
        picks = jnp.concatenate([e_all[2 * i] + e_all[2 * i + 1] for i in range(N_SUB // 2)], axis=1)
        coarse[...] = dot(picks, hot[...]).astype(BF)

    def local_apply(matrix, blocks, d):
        return fold(dot(matrix[zone(d), :], blocks))

    def precondition(k, e, during):
        copies = coarse_send(k)
        if k == 0:
            e_copies = coarse_setup()
            load_l.wait()
        blocks = xw[k]
        for d in range(4):
            loc[zone(d), :] = local_apply(linv, blocks, d)
        during()
        if k == 0:
            coarse_finish(e_copies)
        for copy in copies:
            copy.wait_recv()
        terms = split(cl_all[k].reshape(NC_ALL, NR))
        picked = split(fold(dot(coarse[...], terms)))
        sends = []
        for d in range(4):
            part = fold(dot(basis[:, zone(d)], picked, ((0,), (0,))))
            sent[e - 1, zone(d), :] = weight[zone(d), :] * (loc[zone(d), :] + part)
            sends.append(send_zone(e, d, sent.at[e - 1, zone(d)], got.at[e - 1]))
        return sends

    def operate(k, e):
        sends = []
        blocks = xz[k]
        for d in range(4):
            sent[e - 1, zone(d), :] = local_apply(schur, blocks, d)
            sends.append(send_zone(e, d, sent.at[e - 1, zone(d)], got.at[e - 1]))
        return sends

    def assembled(e, sends, d):
        sends[d ^ 1].wait_recv()
        return sent[e - 1, zone(d), :] + fold(dot(perm[d], split(got[e - 1, d])))

    def finish_z(k, e, sends):
        for d in (2, 3, 0, 1):
            xz[k, zone(d), :] = split(assembled(e, sends, d))

    def finish_q(k, e, sends):
        for d in (2, 3, 0, 1):
            xw[k + 1, zone(d), :] = split(weight[zone(d), :] * assembled(e, sends, d))

    def reduce_start(i):
        share = AR_ROWS[i] // N_GROUP
        copies = []
        for k in range(1, N_GROUP):
            src = ar_in[i].at[pl.ds(pl.multiple_of(share * peers[k - 1][0], 8), share)]
            copies.append(
                remote(src, ar_r1[i].at[g], as1.at[i, k], ar1.at[i, k], peers[k - 1])
            )
        ar_r1[i][g] = ar_in[i][pl.ds(pl.multiple_of(share * g, 8), share), :]
        return copies

    def reduce_spread(i, step, total, targets, send_sem, recv_sem):
        ar_p[i][step] = total
        slot = (lax.div(s, 1), lax.rem(s, 4), lax.div(s, 4))[step]
        copies = [
            remote(ar_p[i].at[step], ar_r2[i].at[step, slot], send_sem.at[i, k], recv_sem.at[i, k], t)
            for k, t in enumerate(targets)
        ]
        ar_r2[i][step, slot] = total
        return copies

    def reduce_sum(i, step, waits, count):
        for copy in waits:
            copy.wait_recv()
        total = ar_r2[i][step, 0]
        for k in range(1, count):
            total = total + ar_r2[i][step, k]
        return total

    def reduce_middle(i, waits):
        for copy in waits:
            copy.wait_recv()
        total = ar_r1[i][0]
        for k in range(1, N_GROUP):
            total = total + ar_r1[i][k]
        if i == 3:
            return reduce_spread(i, 0, total, mates, as2, ar2)
        return reduce_spread(i, 1, total, mates_y, as2, ar2)

    def reduce_more(i, waits):
        return reduce_spread(i, 2, reduce_sum(i, 1, waits, 4), mates_z, as4, ar4)

    def reduce_last(i, waits):
        share = AR_ROWS[i] // N_GROUP
        total = reduce_sum(i, 0, waits, N_SUB) if i == 3 else reduce_sum(i, 2, waits, 4)
        ar_q[i][...] = total
        mine = pl.ds(pl.multiple_of(share * g, 8), share)
        copies = [
            remote(ar_q[i], ar_out[i].at[mine], as3.at[i, k], ar3.at[i, k], peers[k - 1])
            for k in range(1, N_GROUP)
        ]
        ar_out[i][mine, :] = total
        return copies

    def reduce_wait(waits):
        for copy in waits:
            copy.wait_recv()

    def nothing():
        pass

    state = {}

    sends = precondition(0, 1, nothing)
    finish_z(0, 1, sends)
    load_s.wait()
    sends = operate(0, 2)
    ar_in[0][0:NR, :] = gram(xz[0], xw[0])
    finish_q(0, 2, sends)
    ar_in[0][NR:, :] = gram(xz[0], xw[1])
    state["a"] = reduce_start(0)

    def during1():
        state["a"] = reduce_middle(0, state["a"])

    sends = precondition(1, 3, during1)
    state["a"] = reduce_more(0, state["a"])
    finish_z(1, 3, sends)
    sends = operate(1, 4)
    state["a"] = reduce_last(0, state["a"])
    ar_in[1][0:NR, :] = gram(xz[1], xw[1])
    finish_q(1, 4, sends)
    ar_in[1][NR:, :] = gram(xz[1], xw[2])
    state["b"] = reduce_start(1)

    def during2():
        reduce_wait(state["a"])
        mu[0] = ar_out[0][0:NR, :]
        inv[0] = sym(ar_out[0][NR:, :])
        invert_steps(inv.at[0], 0, 64)
        state["b"] = reduce_middle(1, state["b"])

    sends = precondition(2, 5, during2)
    state["b"] = reduce_more(1, state["b"])
    invert_steps(inv.at[0], 64, 128)
    finish_z(2, 5, sends)
    sends = operate(2, 6)
    state["b"] = reduce_last(1, state["b"])
    ar_in[2][...] = gram(xz[2], xw[2])
    state["c"] = reduce_start(2)
    reduce_wait(state["b"])
    m2 = sym(ar_out[1][0:NR, :])
    m3 = sym(ar_out[1][NR:, :])
    inv1 = inv[0]
    t2 = small(inv1, m2)
    inv[1] = sym(m3 - small(m2, t2))
    finish_q(2, 6, sends)
    ar_in[3][...] = gram(xz[2], xw[3])
    state["d"] = reduce_start(3)
    state["c"] = reduce_middle(2, state["c"])
    m0 = mu[0]
    t0 = small(inv1, m0)
    t3 = small(inv1, m3)
    h1 = sym(ar_out[0][NR:, :]) - small(m2, t0)
    state["d"] = reduce_middle(3, state["d"])
    state["c"] = reduce_more(2, state["c"])
    invert_steps(inv.at[1], 0, 64)
    state["d"] = reduce_last(3, state["d"])
    state["c"] = reduce_last(2, state["c"])
    invert_steps(inv.at[1], 64, 128)
    reduce_wait(state["c"])
    m4 = sym(ar_out[2][...])
    inv2 = inv[1]
    s23 = m4 - small(m2, t3)
    y = small(inv2, s23)
    u1 = small(inv2, h1)
    h2 = m2 - small(m3, t0) - lax.dot_general(
        s23, u1, (((0,), (0,)), ((), ())), precision=lax.Precision.HIGHEST, preferred_element_type=F32
    )
    part = small(m3, t3) + lax.dot_general(
        s23, y, (((0,), (0,)), ((), ())), precision=lax.Precision.HIGHEST, preferred_element_type=F32
    )
    a0 = t0 - small(t2, u1)
    d0 = small(t2, y) - t3
    x_out[...] = combine(xz[0], a0) + combine(xz[1], u1)
    xd = xz[2]
    base[0] = split(
        xd[:, :NR].astype(F32) + xd[:, NR:].astype(F32) - combine(xz[1], y) + combine(xz[0], d0)
    )
    r_out[...] = r0[...] - mult[...] * (combine(xw[1], a0) + combine(xw[2], u1))
    qd = xw[3]
    base[1] = split(
        qd[:, :NR].astype(F32) + qd[:, NR:].astype(F32) - combine(xw[2], y) + combine(xw[1], d0)
    )
    reduce_wait(state["d"])
    inv[2] = sym(ar_out[3][...] - part)
    invert_steps(inv.at[2], 0, 128)
    c2 = small(inv[2], h2)
    x_out[...] = x_out[...] + combine(base[0], c2)
    r_out[...] = r_out[...] - mult[...] * combine(base[1], c2)
    for copy in started:
        copy.wait_send()


def shards(
    schur, local_inverse, rhs_parts, basis, coarse_map, coarse_inverse, shared_rows, shared_counts
):
    vmem = pl.BlockSpec(memory_space=pltpu.VMEM)
    anywhere = pl.BlockSpec(memory_space=pl.ANY)
    dma = pltpu.SemaphoreType.DMA
    ar_shapes = [r // N_GROUP for r in AR_ROWS]
    scratch = [
        pltpu.VMEM((NL, NL), BF),
        pltpu.VMEM((NL, NL), BF),
        pltpu.VMEM((NL, NR), BF),
        pltpu.VMEM((NC, NL), BF),
        pltpu.VMEM((1, NC), jnp.int32),
        pltpu.VMEM((OWN_ROWS, NL), BF),
        pltpu.VMEM((2, 4, ZONE), jnp.int32),
        pltpu.VMEM((1, 4), jnp.int32),
        pltpu.VMEM((4, ZONE, ZONE), BF),
        pltpu.VMEM((NL, NR), F32),
        pltpu.VMEM((NL, NR), F32),
        pltpu.VMEM((6, NL, NR), F32),
        pltpu.VMEM((4, ZONE, NR), BF),
        pltpu.VMEM((6, 4, ZONE, NR), F32),
        pltpu.VMEM((NL, NR), F32),
        pltpu.VMEM((4, NL, 2 * NR), BF),
        pltpu.VMEM((3, NL, 2 * NR), BF),
        pltpu.VMEM((NL, NR), F32),
        pltpu.VMEM((2, NL, 2 * NR), BF),
        pltpu.VMEM((3, NC, NR), F32),
        pltpu.VMEM((3, N_SUB, NC, NR), F32),
        pltpu.VMEM((8, NR), jnp.int32),
        pltpu.VMEM((N_SUB, 8, NR), jnp.int32),
        pltpu.VMEM((NL, NC_ALL), BF),
        pltpu.VMEM((N_SUB, NC, NR), BF),
        pltpu.VMEM((N_SUB, NC, NR), BF),
        pltpu.VMEM((NC, NC_ALL), BF),
        pltpu.VMEM((1, NR, NR), F32),
        pltpu.VMEM((3, NR, NR), F32),
        [pltpu.VMEM((r, NR), F32) for r in AR_ROWS],
        [pltpu.VMEM((N_GROUP, r, NR), F32) for r in ar_shapes],
        [pltpu.VMEM((3, r, NR), F32) for r in ar_shapes],
        [pltpu.VMEM((3, N_SUB, r, NR), F32) for r in ar_shapes],
        [pltpu.VMEM((r, NR), F32) for r in ar_shapes],
        [pltpu.VMEM((r, NR), F32) for r in AR_ROWS],
        dma((8,)),
        dma((7, 4)),
        dma((7, 4)),
        dma((3, N_SUB)),
        dma((3, N_SUB)),
        dma((N_SUB,)),
        dma((N_SUB,)),
        dma((N_SUB,)),
        dma((N_SUB,)),
        dma((4, N_GROUP)),
        dma((4, N_GROUP)),
        dma((4, N_SUB)),
        dma((4, N_SUB)),
        dma((4, N_GROUP)),
        dma((4, N_GROUP)),
        dma((4, 4)),
        dma((4, 4)),
    ]
    out = jax.ShapeDtypeStruct((NL, NR), F32)
    x, r = pl.pallas_call(
        kernel,
        out_shape=(out, out),
        in_specs=[anywhere] * 8,
        out_specs=(vmem, vmem),
        scratch_shapes=scratch,
        compiler_params=pltpu.CompilerParams(
            collective_id=0, has_side_effects=True, vmem_limit_bytes=62 * 1024 * 1024
        ),
        name="block_cg",
    )(
        schur[0, 0], local_inverse[0, 0], rhs_parts[0, 0], basis[0, 0], coarse_map[0],
        coarse_inverse[0], shared_rows[0, 0], shared_counts[0],
    )
    return x[None, None], r[None, None]


def solution(mesh):
    placed = (
        P("group", "sub", None, None),
        P("group", "sub", None, None),
        P("group", "sub", None, None),
        P("group", "sub", None, None),
        P("group", "sub", None),
        P("group", "sub", None),
        P("group", "sub", None, None, None),
        P("group", "sub", None),
    )
    return jax.shard_map(
        shards,
        mesh=mesh,
        in_specs=placed,
        out_specs=(P("group", "sub", None, None), P("group", "sub", None, None)),
        check_vma=False,
    )
```

```python
import functools

import jax
import jax.numpy as jnp
from jax import lax
from jax.experimental import pallas as pl
from jax.experimental.pallas import tpu as pltpu
from jax.sharding import PartitionSpec as P

BF = jnp.bfloat16
F32 = jnp.float32
MESH = pl.DeviceIdType.MESH
N_GROUP = 8
N_SUB = 16
NL = 1024
ZONE = 256
NR = 128
NC = 32
NC_ALL = NC * N_SUB
OWN_ROWS = 64
HALF = NR // 2
AR_ROWS = (256, 256, 128, 128)


def split(x):
    hi = x.astype(BF)
    lo = (x - hi.astype(F32)).astype(BF)
    return jnp.concatenate([hi, lo], axis=-1)


def fold(y):
    return y[:, :NR] + y[:, NR:]


def dot(a, b, dims=((1,), (0,))):
    return lax.dot_general(a, b, (dims, ((), ())), preferred_element_type=F32)


def small(a, b):
    return jnp.dot(a, b, precision=lax.Precision.HIGHEST, preferred_element_type=F32)


def gram(left, right):
    full = dot(left, right, ((0,), (0,)))
    half = full[:NR] + full[NR:]
    return half[:, :NR] + half[:, NR:]


def sym(a):
    return 0.5 * (a + a.T)


def combine(blocks, mixing):
    halves = split(mixing)
    return fold(dot(blocks, jnp.concatenate([halves, halves], axis=0)))


def invert_steps(mat, first, last):
    lane = lax.broadcasted_iota(jnp.int32, (HALF, NR), 1)
    sub = lax.broadcasted_iota(jnp.int32, (HALF, NR), 0)
    lane8 = lax.broadcasted_iota(jnp.int32, (8, NR), 1)

    def column(a, lanes, j):
        return jnp.broadcast_to(
            jnp.sum(jnp.where(lanes == j, a, 0.0), axis=1, keepdims=True), a.shape
        )

    def step(i, carry):
        k = 4 * i
        a = mat[...]
        r = [jnp.broadcast_to(mat[pl.ds(k + j, 1), :], (8, NR)) for j in range(4)]
        c = [column(a, lane, k + j) for j in range(4)]
        d = [[column(r[m], lane8, k + j) for j in range(4)] for m in range(4)]
        inside = (lane8 >= k) & (lane8 < k + 4)
        q = [jnp.where(lane8 == k + j, 1.0, jnp.where(inside, 0.0, r[j])) for j in range(4)]
        i0 = 1.0 / (d[0][0] * d[1][1] - d[0][1] * d[1][0])

        def lead(x0, x1):
            return (d[1][1] * x0 - d[0][1] * x1) * i0, (d[0][0] * x1 - d[1][0] * x0) * i0

        e02, e12 = lead(d[0][2], d[1][2])
        e03, e13 = lead(d[0][3], d[1][3])
        f0, f1 = lead(q[0], q[1])
        s22 = d[2][2] - d[2][0] * e02 - d[2][1] * e12
        s23 = d[2][3] - d[2][0] * e03 - d[2][1] * e13
        s32 = d[3][2] - d[3][0] * e02 - d[3][1] * e12
        s33 = d[3][3] - d[3][0] * e03 - d[3][1] * e13
        g2 = q[2] - d[2][0] * f0 - d[2][1] * f1
        g3 = q[3] - d[3][0] * f0 - d[3][1] * f1
        i1 = 1.0 / (s22 * s33 - s23 * s32)
        w2 = (s33 * g2 - s23 * g3) * i1
        w3 = (s22 * g3 - s32 * g2) * i1
        w = [f0 - e02 * w2 - e03 * w3, f1 - e12 * w2 - e13 * w3, w2, w3]
        w = [x[0:1] for x in w]
        new = jnp.where((lane >= k) & (lane < k + 4), 0.0, a)
        new = new - (c[0] * w[0] + c[1] * w[1]) - (c[2] * w[2] + c[3] * w[3])
        for j in range(4):
            new = jnp.where(sub == k + j, w[j], new)
        mat[...] = new
        return carry

    lax.fori_loop(first // 4, last // 4, step, 0)


def small_t(a, b):
    return lax.dot_general(
        a, b, (((0,), (0,)), ((), ())), precision=lax.Precision.HIGHEST, preferred_element_type=F32
    )


def invert_lead(top, mat):
    top[...] = mat[0:HALF, :]


def invert_next(top, bottom, mat):
    rest = mat[HALF:, HALF:] - small_t(mat[0:HALF, HALF:], top[:, HALF:])
    bottom[...] = jnp.concatenate([rest, jnp.zeros((HALF, HALF), F32)], axis=1)


def invert_end(top, bottom):
    x = top[:, HALF:]
    low = bottom[:, :HALF]
    xl = small(x, low)
    corner = top[:, :HALF] + lax.dot_general(
        xl, x, (((1,), (1,)), ((), ())), precision=lax.Precision.HIGHEST, preferred_element_type=F32
    )
    upper = jnp.concatenate([corner, -xl], axis=1)
    lower = jnp.concatenate([-xl.T, low], axis=1)
    return jnp.concatenate([upper, lower], axis=0)


def kernel(
    schur_h, linv_h, rhs_h, basis_h, cmap_h, cinv_h, rows_h, counts_h,
    x_out, r_out,
    schur, linv, rhs, basis, cmap, cinv, rows, counts, perm, weight, mult, sent, got0, got, r0, xw, xz, loc, base,
    cl_mine, cl_all, map_mine, map_all, hot, e_mine, e_all, coarse, mat, top, bottom, g_mine, g_all, ct_mine, ct_all, pk_mine, pk_all,
    ar_in, ar_r1, ar_p, ar_r2, ar_q, ar_out,
    load_sem, xs, xr, cs, cr, ms, mr, es, er, as1, ar1, as2, ar2, as3, ar3, as4, ar4, gs, gr, ts, tr, ps, pr,
):
    g = lax.axis_index("group")
    s = lax.axis_index("sub")
    started = []

    def remote(src, dst, send_sem, recv_sem, target):
        copy = pltpu.make_async_remote_copy(
            src_ref=src, dst_ref=dst, send_sem=send_sem, recv_sem=recv_sem,
            device_id=target, device_id_type=MESH,
        )
        copy.start()

    def arrived(span, sem):
        pltpu.make_async_copy(span, span, sem).wait()

    def transfer(copies, span, send_sem, recv_sem):
        for src, dst, target in copies:
            remote(src, dst, send_sem, recv_sem, target)
        started.append((span, send_sem))
        return span, recv_sem

    pairs = (
        (cmap_h, cmap), (rhs_h, rhs), (rows_h, rows), (counts_h, counts),
        (basis_h, basis), (cinv_h, cinv), (linv_h, linv), (schur_h, schur),
    )
    loads = [pltpu.make_async_copy(a, b, load_sem.at[i]) for i, (a, b) in enumerate(pairs)]
    for load in loads:
        load.start()
    load_l, load_s = loads[6:]

    barrier = pltpu.get_barrier_semaphore()
    mates = [(g, lax.rem(s + k, N_SUB)) for k in range(1, N_SUB)]
    peers = [(lax.rem(g + k, N_GROUP), s) for k in range(1, N_GROUP)]
    y, z = lax.rem(s, 4), lax.div(s, 4)
    mates_y = [(g, 4 * z + lax.rem(y + k, 4)) for k in range(1, 4)]
    mates_z = [(g, 4 * lax.rem(z + k, 4) + y) for k in range(1, 4)]
    for target in mates + peers:
        pl.semaphore_signal(barrier, inc=1, device_id=target, device_id_type=MESH)

    map_mine[...] = jnp.zeros((8, NR), jnp.int32)
    loads[0].wait()
    map_mine[0:1, 0:NC] = cmap[...]
    tile = jnp.broadcast_to(map_mine[0:1, :], (8, NR))
    tile = pltpu.roll(tile, NC * lax.rem(s, 4), 1)
    at_row = lax.broadcasted_iota(jnp.int32, (8, NR), 0) == lax.div(s, 4)
    map_mine[...] = jnp.where(at_row, tile, 0)

    for load in loads[1:6]:
        load.wait()
    pl.semaphore_wait(barrier, len(mates) + len(peers))

    around = [
        (g, lax.rem(s + 1, N_SUB)),
        (g, lax.rem(s + N_SUB - 1, N_SUB)),
        (lax.rem(g + 1, N_GROUP), s),
        (lax.rem(g + N_GROUP - 1, N_GROUP), s),
    ]

    def send_zone(e, d, src, dst):
        remote(src, dst.at[d ^ 1], xs.at[e], xr.at[e, d ^ 1], around[d])
        if d == 3:
            started.append((dst, xs.at[e]))

    def zone_arrived(e, d):
        zones = got0 if e == 0 else got.at[e - 1]
        arrived(zones.at[d], xr.at[e, d])

    def zone(d):
        return pl.ds(ZONE * d, ZONE)

    for d in range(4):
        send_zone(0, d, rhs.at[zone(d)], got0)
    map_sent = transfer(
        [(map_mine, map_all.at[k], mates[k - 1]) for k in range(1, N_SUB)],
        map_all.at[pl.ds(0, N_SUB - 1)], ms.at[0], mr.at[0],
    )

    lane = lax.broadcasted_iota(jnp.int32, (1, ZONE), 1)
    at = lax.broadcasted_iota(jnp.int32, (ZONE, ZONE), 0)
    for d in range(4):
        mine = jnp.where(lane < counts[0:1, d : d + 1], rows[0, d : d + 1, :] - ZONE * d, -1)
        theirs = rows[1, d : d + 1, :] - ZONE * (d ^ 1)
        place = jnp.where(at == mine, 1.0, 0.0)
        times = 1.0 + jnp.sum(place, axis=1, keepdims=True)
        mult[zone(d), :] = jnp.broadcast_to(times, (ZONE, NR))
        weight[zone(d), :] = jnp.broadcast_to(1.0 / times, (ZONE, NR))
        pick = jnp.where(at == theirs, 1.0, 0.0).astype(BF)
        pairs_d = dot(place.astype(BF), pick, ((1,), (1,)))
        perm[d] = pairs_d.astype(BF)
        shared = (pairs_d * (1.0 / times)).astype(BF)
        g_mine[d] = dot(basis[:, zone(d)], shared).astype(BF)
    g_sent = transfer(
        [(g_mine.at[d], g_all.at[d ^ 1], around[d]) for d in range(4)], g_all, gs.at[0], gr.at[0]
    )

    for d in (2, 3, 0, 1):
        zone_arrived(0, d)
        block = rhs[zone(d), :].astype(F32) + dot(perm[d], got0[d])
        r0[zone(d), :] = block
        xw[0, zone(d), :] = split(weight[zone(d), :] * block)

    def coarse_send(k, local):
        cl_mine[k] = local
        cl_all[k, s] = local
        return transfer(
            [(cl_mine.at[k], cl_all.at[k, s], t) for t in mates],
            cl_all.at[k, pl.ds(0, N_SUB - 1)], cs.at[k], cr.at[k],
        )

    def coarse_setup():
        arrived(*map_sent)
        total = map_mine[...]
        for k in range(1, N_SUB):
            total = total + map_all[k]
        at_all = lax.broadcasted_iota(jnp.int32, (NL, NR), 0)
        for i in range(4):
            hot[:, NR * i : NR * (i + 1)] = jnp.where(
                at_all == total[i : i + 1, :], 1.0, 0.0
            ).astype(BF)
        picks = dot(cinv[...], hot[...]).T
        picks = jnp.concatenate([picks, picks], axis=1)
        half = lax.broadcasted_iota(jnp.int32, (NC_ALL, NR), 1) // OWN_ROWS
        picks = jnp.where(half == lax.rem(s, 2), picks, 0.0).astype(BF)
        e_mine[...] = picks.reshape(N_SUB, NC, NR)
        e_all[s] = e_mine[s]
        return transfer(
            [
                (e_mine.at[lax.rem(s + k, N_SUB)], e_all.at[s], mates[k - 1])
                for k in range(1, N_SUB)
            ],
            e_all.at[pl.ds(0, N_SUB - 1)], es.at[0], er.at[0],
        )

    def coarse_finish(e_sent):
        arrived(*e_sent)
        picks = jnp.concatenate([e_all[2 * i] + e_all[2 * i + 1] for i in range(N_SUB // 2)], axis=1)
        coarse[...] = dot(picks, hot[...]).astype(BF)

    def local_apply(matrix, blocks, d):
        return fold(dot(matrix[zone(d), :], blocks))

    def local_part(k, e):
        blocks = xw[k]
        for d in range(4):
            sent[e - 1, zone(d), :] = weight[zone(d), :] * local_apply(linv, blocks, d)
            send_zone(e, d, sent.at[e - 1, zone(d)], got.at[e - 1])

    def coarse_part(k, e, gathered):
        arrived(*gathered)
        terms = split(cl_all[k].reshape(NC_ALL, NR))
        values = fold(dot(coarse[...], terms))
        pk_mine[k] = values
        values_sent = transfer(
            [(pk_mine.at[k], pk_all.at[k, d ^ 1], around[d]) for d in range(4)],
            pk_all.at[k], ps.at[k], pr.at[k],
        )
        picked = split(values)
        for d in range(4):
            part = fold(dot(basis[:, zone(d)], picked, ((0,), (0,))))
            loc[zone(d), :] = sent[e - 1, zone(d), :] + weight[zone(d), :] * part
        return values_sent

    def finish_z(k, e, values_sent):
        arrived(*values_sent)
        for d in (2, 3, 0, 1):
            theirs = fold(dot(g_all[d], split(pk_all[k, d]), ((0,), (0,))))
            mine = loc[zone(d), :] + theirs
            zone_arrived(e, d)
            xz[k, zone(d), :] = split(mine + fold(dot(perm[d], split(got[e - 1, d]))))

    def operate(k, e, coarse_too):
        blocks = xz[k]
        for d in range(4):
            image = local_apply(schur, blocks, d)
            sent[e - 1, zone(d), :] = image
            if coarse_too:
                ct_mine[k, d] = fold(dot(g_all[d], split(image)))
                remote(ct_mine.at[k, d], ct_all.at[k, d ^ 1], ts.at[k], tr.at[k], around[d])
            send_zone(e, d, sent.at[e - 1, zone(d)], got.at[e - 1])
        if coarse_too:
            started.append((ct_all.at[k], ts.at[k]))

    def coarse_shares(k, e):
        total = fold(dot(basis[...], split(weight[...] * sent[e - 1])))
        arrived(ct_all.at[k], tr.at[k])
        for d in range(4):
            total = total + ct_all[k, d]
        return coarse_send(k + 1, total)

    def finish_q(k, e):
        for d in (2, 3, 0, 1):
            zone_arrived(e, d)
            whole = sent[e - 1, zone(d), :] + fold(dot(perm[d], split(got[e - 1, d])))
            xw[k + 1, zone(d), :] = split(weight[zone(d), :] * whole)

    def reduce_start(i):
        share = AR_ROWS[i] // N_GROUP

        def part(t):
            return pl.ds(pl.multiple_of(share * t, 8), share)

        ar_r1[i][g] = ar_in[i][part(g), :]
        return transfer(
            [(ar_in[i].at[part(t[0])], ar_r1[i].at[g], t) for t in peers],
            ar_r1[i].at[pl.ds(0, N_GROUP - 1)], as1.at[i], ar1.at[i],
        )

    def reduce_spread(i, step, total, targets, send_sem, recv_sem):
        ar_p[i][step] = total
        slot = (s, lax.rem(s, 4), lax.div(s, 4))[step]
        ar_r2[i][step, slot] = total
        return transfer(
            [(ar_p[i].at[step], ar_r2[i].at[step, slot], t) for t in targets],
            ar_r2[i].at[step, pl.ds(0, len(targets))], send_sem.at[i], recv_sem.at[i],
        )

    def reduce_sum(i, step, waits, count):
        arrived(*waits)
        total = ar_r2[i][step, 0]
        for k in range(1, count):
            total = total + ar_r2[i][step, k]
        return total

    def reduce_middle(i, waits):
        arrived(*waits)
        total = ar_r1[i][0]
        for k in range(1, N_GROUP):
            total = total + ar_r1[i][k]
        if i == 3:
            return reduce_spread(i, 0, total, mates, as2, ar2)
        return reduce_spread(i, 1, total, mates_y, as2, ar2)

    def reduce_more(i, waits):
        return reduce_spread(i, 2, reduce_sum(i, 1, waits, 4), mates_z, as4, ar4)

    def reduce_last(i, waits):
        share = AR_ROWS[i] // N_GROUP
        total = reduce_sum(i, 0, waits, N_SUB) if i == 3 else reduce_sum(i, 2, waits, 4)
        ar_q[i][...] = total
        mine = pl.ds(pl.multiple_of(share * g, 8), share)
        ar_out[i][mine, :] = total
        return transfer(
            [(ar_q[i], ar_out[i].at[mine], t) for t in peers],
            ar_out[i].at[pl.ds(0, share * (N_GROUP - 1))], as3.at[i], ar3.at[i],
        )

    def reduce_wait(waits):
        arrived(*waits)

    gathered = coarse_send(0, fold(dot(basis[...], xw[0])))
    e_sent = coarse_setup()
    load_l.wait()
    local_part(0, 1)
    arrived(*g_sent)
    coarse_finish(e_sent)
    values_sent = coarse_part(0, 1, gathered)
    load_s.wait()
    finish_z(0, 1, values_sent)

    operate(0, 2, True)
    gathered = coarse_shares(0, 2)
    ar_in[0][0:NR, :] = gram(xz[0], xw[0])
    finish_q(0, 2)
    local_part(1, 3)
    ar_in[0][NR:, :] = gram(xz[0], xw[1])
    ar_a = reduce_start(0)
    values_sent = coarse_part(1, 3, gathered)
    ar_a = reduce_middle(0, ar_a)
    finish_z(1, 3, values_sent)

    operate(1, 4, True)
    ar_a = reduce_more(0, ar_a)
    gathered = coarse_shares(1, 4)
    ar_in[1][0:NR, :] = gram(xz[1], xw[1])
    ar_a = reduce_last(0, ar_a)
    finish_q(1, 4)
    local_part(2, 5)
    ar_in[1][NR:, :] = gram(xz[1], xw[2])
    ar_b = reduce_start(1)
    reduce_wait(ar_a)
    mat[0] = sym(ar_out[0][NR:, :])
    invert_lead(top.at[0], mat.at[0])
    invert_steps(top.at[0], 0, 32)
    values_sent = coarse_part(2, 5, gathered)
    ar_b = reduce_middle(1, ar_b)
    invert_steps(top.at[0], 32, 64)
    invert_next(top.at[0], bottom.at[0], mat.at[0])
    finish_z(2, 5, values_sent)

    operate(2, 6, False)
    ar_in[2][...] = gram(xz[2], xw[2])
    ar_c = reduce_start(2)
    ar_b = reduce_more(1, ar_b)
    invert_steps(bottom.at[0], 0, 64)
    inv1 = invert_end(top.at[0], bottom.at[0])
    m0 = ar_out[0][0:NR, :]
    ar_b = reduce_last(1, ar_b)
    t0 = small(inv1, m0)
    finish_q(2, 6)
    ar_in[3][...] = gram(xz[2], xw[3])
    ar_d = reduce_start(3)
    ar_c = reduce_middle(2, ar_c)
    reduce_wait(ar_b)
    m2 = sym(ar_out[1][0:NR, :])
    m3 = sym(ar_out[1][NR:, :])
    t2 = small(inv1, m2)
    mat[1] = sym(m3 - small(m2, t2))
    invert_lead(top.at[1], mat.at[1])
    ar_d = reduce_middle(3, ar_d)
    ar_c = reduce_more(2, ar_c)
    invert_steps(top.at[1], 0, 64)
    invert_next(top.at[1], bottom.at[1], mat.at[1])
    ar_c = reduce_last(2, ar_c)
    invert_steps(bottom.at[1], 0, 32)
    ar_d = reduce_last(3, ar_d)
    invert_steps(bottom.at[1], 32, 64)
    inv2 = invert_end(top.at[1], bottom.at[1])
    t3 = small(inv1, m3)
    h1 = mat[0] - small(m2, t0)
    reduce_wait(ar_c)
    m4 = sym(ar_out[2][...])
    s23 = m4 - small(m2, t3)
    y = small(inv2, s23)
    u1 = small(inv2, h1)
    h2 = m2 - small(m3, t0) - small_t(s23, u1)
    part = small(m3, t3) + small_t(s23, y)
    a0 = t0 - small(t2, u1)
    d0 = small(t2, y) - t3
    x_out[...] = combine(xz[0], a0) + combine(xz[1], u1)
    xd = xz[2]
    base[0] = split(
        xd[:, :NR].astype(F32) + xd[:, NR:].astype(F32) - combine(xz[1], y) + combine(xz[0], d0)
    )
    r_out[...] = r0[...] - mult[...] * (combine(xw[1], a0) + combine(xw[2], u1))
    qd = xw[3]
    base[1] = split(
        qd[:, :NR].astype(F32) + qd[:, NR:].astype(F32) - combine(xw[2], y) + combine(xw[1], d0)
    )
    reduce_wait(ar_d)
    mat[2] = sym(ar_out[3][...] - part)
    invert_lead(top.at[2], mat.at[2])
    invert_steps(top.at[2], 0, 64)
    invert_next(top.at[2], bottom.at[2], mat.at[2])
    cross = top[2, :, HALF:]
    above = small(top[2, :, :HALF], h2[:HALF])
    below = h2[HALF:] - small_t(cross, h2[:HALF])
    invert_steps(bottom.at[2], 0, 64)
    below = small(bottom[2, :, :HALF], below)
    c2 = jnp.concatenate([above - small(cross, below), below], axis=0)
    x_out[...] = x_out[...] + combine(base[0], c2)
    r_out[...] = r_out[...] - mult[...] * combine(base[1], c2)
    for span, sem in started:
        arrived(span, sem)


def shards(
    schur, local_inverse, rhs_parts, basis, coarse_map, coarse_inverse, shared_rows, shared_counts
):
    vmem = pl.BlockSpec(memory_space=pltpu.VMEM)
    in_hbm = pl.BlockSpec(memory_space=pl.ANY)
    dma = pltpu.SemaphoreType.DMA
    ar_shapes = [r // N_GROUP for r in AR_ROWS]
    scratch = [
        pltpu.VMEM((NL, NL), BF),
        pltpu.VMEM((NL, NL), BF),
        pltpu.VMEM((NL, NR), BF),
        pltpu.VMEM((NC, NL), BF),
        pltpu.VMEM((1, NC), jnp.int32),
        pltpu.VMEM((OWN_ROWS, NL), BF),
        pltpu.VMEM((2, 4, ZONE), jnp.int32),
        pltpu.VMEM((1, 4), jnp.int32),
        pltpu.VMEM((4, ZONE, ZONE), BF),
        pltpu.VMEM((NL, NR), F32),
        pltpu.VMEM((NL, NR), F32),
        pltpu.VMEM((6, NL, NR), F32),
        pltpu.VMEM((4, ZONE, NR), BF),
        pltpu.VMEM((6, 4, ZONE, NR), F32),
        pltpu.VMEM((NL, NR), F32),
        pltpu.VMEM((4, NL, 2 * NR), BF),
        pltpu.VMEM((3, NL, 2 * NR), BF),
        pltpu.VMEM((NL, NR), F32),
        pltpu.VMEM((2, NL, 2 * NR), BF),
        pltpu.VMEM((3, NC, NR), F32),
        pltpu.VMEM((3, N_SUB, NC, NR), F32),
        pltpu.VMEM((8, NR), jnp.int32),
        pltpu.VMEM((N_SUB, 8, NR), jnp.int32),
        pltpu.VMEM((NL, NC_ALL), BF),
        pltpu.VMEM((N_SUB, NC, NR), BF),
        pltpu.VMEM((N_SUB, NC, NR), BF),
        pltpu.VMEM((NC, NC_ALL), BF),
        pltpu.VMEM((3, NR, NR), F32),
        pltpu.VMEM((3, HALF, NR), F32),
        pltpu.VMEM((3, HALF, NR), F32),
        pltpu.VMEM((4, NC, ZONE), BF),
        pltpu.VMEM((4, NC, ZONE), BF),
        pltpu.VMEM((2, 4, NC, NR), F32),
        pltpu.VMEM((2, 4, NC, NR), F32),
        pltpu.VMEM((3, NC, NR), F32),
        pltpu.VMEM((3, 4, NC, NR), F32),
        [pltpu.VMEM((r, NR), F32) for r in AR_ROWS],
        [pltpu.VMEM((N_GROUP, r, NR), F32) for r in ar_shapes],
        [pltpu.VMEM((3, r, NR), F32) for r in ar_shapes],
        [pltpu.VMEM((3, N_SUB, r, NR), F32) for r in ar_shapes],
        [pltpu.VMEM((r, NR), F32) for r in ar_shapes],
        [pltpu.VMEM((r, NR), F32) for r in AR_ROWS],
        dma((8,)),
        dma((7,)),
        dma((7, 4)),
        dma((3,)),
        dma((3,)),
        dma((1,)),
        dma((1,)),
        dma((1,)),
        dma((1,)),
        dma((4,)),
        dma((4,)),
        dma((4,)),
        dma((4,)),
        dma((4,)),
        dma((4,)),
        dma((4,)),
        dma((4,)),
        dma((1,)),
        dma((1,)),
        dma((2,)),
        dma((2,)),
        dma((3,)),
        dma((3,)),
    ]
    out = jax.ShapeDtypeStruct((NL, NR), F32)
    x, r = pl.pallas_call(
        kernel,
        out_shape=(out, out),
        in_specs=[in_hbm] * 8,
        out_specs=(vmem, vmem),
        scratch_shapes=scratch,
        compiler_params=pltpu.CompilerParams(
            collective_id=0, has_side_effects=True, vmem_limit_bytes=62 * 1024 * 1024
        ),
        name="block_cg",
    )(
        schur[0, 0], local_inverse[0, 0], rhs_parts[0, 0], basis[0, 0], coarse_map[0],
        coarse_inverse[0], shared_rows[0, 0], shared_counts[0],
    )
    return x[None, None], r[None, None]


def solution(mesh):
    placed = (
        P("group", "sub", None, None),
        P("group", "sub", None, None),
        P("group", "sub", None, None),
        P("group", "sub", None, None),
        P("group", "sub", None),
        P("group", "sub", None),
        P("group", "sub", None, None, None),
        P("group", "sub", None),
    )
    return jax.shard_map(
        shards,
        mesh=mesh,
        in_specs=placed,
        out_specs=(P("group", "sub", None, None), P("group", "sub", None, None)),
        check_vma=False,
    )
```

```python
import functools

import jax
import jax.numpy as jnp
from jax import lax
from jax.experimental import pallas as pl
from jax.experimental.pallas import tpu as pltpu
from jax.sharding import PartitionSpec as P

BF = jnp.bfloat16
F32 = jnp.float32
MESH = pl.DeviceIdType.MESH
N_GROUP = 8
N_SUB = 16
NL = 1024
ZONE = 256
NR = 128
NC = 32
NC_ALL = NC * N_SUB
OWN_ROWS = 64
HALF = NR // 2
AR_ROWS = (256, 256, 128, 128)


def split(x):
    hi = x.astype(BF)
    lo = (x - hi.astype(F32)).astype(BF)
    return jnp.concatenate([hi, lo], axis=-1)


def fold(y):
    return y[:, :NR] + y[:, NR:]


def dot(a, b, dims=((1,), (0,))):
    return lax.dot_general(a, b, (dims, ((), ())), preferred_element_type=F32)


def small(a, b):
    return jnp.dot(a, b, precision=lax.Precision.HIGHEST, preferred_element_type=F32)


def gram(left, right):
    full = dot(left, right, ((0,), (0,)))
    half = full[:NR] + full[NR:]
    return half[:, :NR] + half[:, NR:]


def sym(a):
    return 0.5 * (a + a.T)


def combine(blocks, mixing):
    halves = split(mixing)
    return fold(dot(blocks, jnp.concatenate([halves, halves], axis=0)))


def invert_steps(mat, first, last):
    lane = lax.broadcasted_iota(jnp.int32, (HALF, NR), 1)
    sub = lax.broadcasted_iota(jnp.int32, (HALF, NR), 0)
    lane8 = lax.broadcasted_iota(jnp.int32, (8, NR), 1)

    def column(a, lanes, j):
        return jnp.broadcast_to(
            jnp.sum(jnp.where(lanes == j, a, 0.0), axis=1, keepdims=True), a.shape
        )

    def step(i, carry):
        k = 4 * i
        a = mat[...]
        r = [jnp.broadcast_to(mat[pl.ds(k + j, 1), :], (8, NR)) for j in range(4)]
        c = [column(a, lane, k + j) for j in range(4)]
        d = [[column(r[m], lane8, k + j) for j in range(4)] for m in range(4)]
        inside = (lane8 >= k) & (lane8 < k + 4)
        q = [jnp.where(lane8 == k + j, 1.0, jnp.where(inside, 0.0, r[j])) for j in range(4)]
        i0 = 1.0 / (d[0][0] * d[1][1] - d[0][1] * d[1][0])

        def lead(x0, x1):
            return (d[1][1] * x0 - d[0][1] * x1) * i0, (d[0][0] * x1 - d[1][0] * x0) * i0

        e02, e12 = lead(d[0][2], d[1][2])
        e03, e13 = lead(d[0][3], d[1][3])
        f0, f1 = lead(q[0], q[1])
        s22 = d[2][2] - d[2][0] * e02 - d[2][1] * e12
        s23 = d[2][3] - d[2][0] * e03 - d[2][1] * e13
        s32 = d[3][2] - d[3][0] * e02 - d[3][1] * e12
        s33 = d[3][3] - d[3][0] * e03 - d[3][1] * e13
        g2 = q[2] - d[2][0] * f0 - d[2][1] * f1
        g3 = q[3] - d[3][0] * f0 - d[3][1] * f1
        i1 = 1.0 / (s22 * s33 - s23 * s32)
        w2 = (s33 * g2 - s23 * g3) * i1
        w3 = (s22 * g3 - s32 * g2) * i1
        w = [f0 - e02 * w2 - e03 * w3, f1 - e12 * w2 - e13 * w3, w2, w3]
        w = [x[0:1] for x in w]
        new = jnp.where((lane >= k) & (lane < k + 4), 0.0, a)
        new = new - (c[0] * w[0] + c[1] * w[1]) - (c[2] * w[2] + c[3] * w[3])
        for j in range(4):
            new = jnp.where(sub == k + j, w[j], new)
        mat[...] = new
        return carry

    lax.fori_loop(first // 4, last // 4, step, 0)


def small_t(a, b):
    return lax.dot_general(
        a, b, (((0,), (0,)), ((), ())), precision=lax.Precision.HIGHEST, preferred_element_type=F32
    )


def invert_lead(top, mat):
    top[...] = mat[0:HALF, :]


def invert_next(top, bottom, mat):
    rest = mat[HALF:, HALF:] - small_t(mat[0:HALF, HALF:], top[:, HALF:])
    bottom[...] = jnp.concatenate([rest, jnp.zeros((HALF, HALF), F32)], axis=1)


def invert_end(top, bottom):
    x = top[:, HALF:]
    low = bottom[:, :HALF]
    xl = small(x, low)
    corner = top[:, :HALF] + lax.dot_general(
        xl, x, (((1,), (1,)), ((), ())), precision=lax.Precision.HIGHEST, preferred_element_type=F32
    )
    upper = jnp.concatenate([corner, -xl], axis=1)
    lower = jnp.concatenate([-xl.T, low], axis=1)
    return jnp.concatenate([upper, lower], axis=0)


def kernel(
    schur_h, linv_h, rhs_h, basis_h, cmap_h, cinv_h, rows_h, counts_h,
    x_out, r_out,
    schur, linv, rhs, basis, cmap, cinv, rows, counts, perm, weight, mult, sent, coded, step_mine, step_all, got0, got, r0, xw, xz, loc, base,
    cl_mine, cl_all, map_mine, map_all, hot, e_mine, e_all, coarse, mat, top, bottom, g_mine, g_all, ct_mine, ct_all, gs_rows, own_share, pk_mine, pk_all,
    ar_in, ar_r1, ar_p, ar_r2, ar_q, ar_out,
    load_sem, xs, xr, cs, cr, ms, mr, es, er, as1, ar1, as2, ar2, as3, ar3, as4, ar4, gs, gr, ts, tr, ps, pr, qs, qr,
):
    g = lax.axis_index("group")
    s = lax.axis_index("sub")
    started = []

    def remote(src, dst, send_sem, recv_sem, target):
        copy = pltpu.make_async_remote_copy(
            src_ref=src, dst_ref=dst, send_sem=send_sem, recv_sem=recv_sem,
            device_id=target, device_id_type=MESH,
        )
        copy.start()

    def arrived(span, sem):
        pltpu.make_async_copy(span, span, sem).wait()

    def transfer(copies, span, send_sem, recv_sem):
        for src, dst, target in copies:
            remote(src, dst, send_sem, recv_sem, target)
        started.append((span, send_sem))
        return span, recv_sem

    pairs = (
        (cmap_h, cmap), (rhs_h, rhs), (rows_h, rows), (counts_h, counts),
        (basis_h, basis), (cinv_h, cinv), (linv_h, linv), (schur_h, schur),
    )
    loads = [pltpu.make_async_copy(a, b, load_sem.at[i]) for i, (a, b) in enumerate(pairs)]
    for load in loads:
        load.start()
    load_l, load_s = loads[6:]

    barrier = pltpu.get_barrier_semaphore()
    mates = [(g, lax.rem(s + k, N_SUB)) for k in range(1, N_SUB)]
    peers = [(lax.rem(g + k, N_GROUP), s) for k in range(1, N_GROUP)]
    y, z = lax.rem(s, 4), lax.div(s, 4)
    mates_y = [(g, 4 * z + lax.rem(y + k, 4)) for k in range(1, 4)]
    mates_z = [(g, 4 * lax.rem(z + k, 4) + y) for k in range(1, 4)]
    for target in mates + peers:
        pl.semaphore_signal(barrier, inc=1, device_id=target, device_id_type=MESH)

    map_mine[...] = jnp.zeros((8, NR), jnp.int32)
    loads[0].wait()
    map_mine[0:1, 0:NC] = cmap[...]
    tile = jnp.broadcast_to(map_mine[0:1, :], (8, NR))
    tile = pltpu.roll(tile, NC * lax.rem(s, 4), 1)
    at_row = lax.broadcasted_iota(jnp.int32, (8, NR), 0) == lax.div(s, 4)
    map_mine[...] = jnp.where(at_row, tile, 0)

    for load in loads[1:6]:
        load.wait()
    pl.semaphore_wait(barrier, len(mates) + len(peers))

    around = [
        (g, lax.rem(s + 1, N_SUB)),
        (g, lax.rem(s + N_SUB - 1, N_SUB)),
        (lax.rem(g + 1, N_GROUP), s),
        (lax.rem(g + N_GROUP - 1, N_GROUP), s),
    ]

    def send_zone(e, d, src, dst):
        remote(src, dst.at[d ^ 1], xs.at[e], xr.at[e, d ^ 1], around[d])
        if d == 3:
            started.append((dst, xs.at[e]))

    def ship(e, d, value):
        sent[e - 1, zone(d), :] = value
        top_value = jnp.maximum(jnp.max(jnp.abs(value), axis=0, keepdims=True), 2e-34)
        step_mine[e - 1, d] = jnp.broadcast_to(top_value * (1.0 / 32767.0), (8, NR))
        remote(
            step_mine.at[e - 1, d], step_all.at[e - 1, d ^ 1], qs.at[e - 1], qr.at[e - 1], around[d]
        )
        if d == 3:
            started.append((step_all.at[e - 1], qs.at[e - 1]))
        steps = jnp.round(value * (32767.0 / top_value))
        coded[e - 1, zone(d), :] = steps.astype(jnp.int32).astype(jnp.int16)
        send_zone(e, d, coded.at[e - 1, zone(d)], got.at[e - 1])

    def steps_arrived(e):
        arrived(step_all.at[e - 1], qr.at[e - 1])

    def shipped(e, d):
        zone_arrived(e, d)
        steps = got[e - 1, d].astype(jnp.int32).astype(F32)
        return fold(dot(perm[d], split(steps))) * step_all[e - 1, d, 0:1, :]

    def zone_arrived(e, d):
        zones = got0 if e == 0 else got.at[e - 1]
        arrived(zones.at[d], xr.at[e, d])

    def zone(d):
        return pl.ds(ZONE * d, ZONE)

    for d in range(4):
        send_zone(0, d, rhs.at[zone(d)], got0)
    map_sent = transfer(
        [(map_mine, map_all.at[k], mates[k - 1]) for k in range(1, N_SUB)],
        map_all.at[pl.ds(0, N_SUB - 1)], ms.at[0], mr.at[0],
    )

    lane = lax.broadcasted_iota(jnp.int32, (1, ZONE), 1)
    at = lax.broadcasted_iota(jnp.int32, (ZONE, ZONE), 0)
    for d in range(4):
        mine = jnp.where(lane < counts[0:1, d : d + 1], rows[0, d : d + 1, :] - ZONE * d, -1)
        theirs = rows[1, d : d + 1, :] - ZONE * (d ^ 1)
        place = jnp.where(at == mine, 1.0, 0.0)
        times = 1.0 + jnp.sum(place, axis=1, keepdims=True)
        mult[zone(d), :] = jnp.broadcast_to(times, (ZONE, NR))
        weight[zone(d), :] = jnp.broadcast_to(1.0 / times, (ZONE, NR))
        pick = jnp.where(at == theirs, 1.0, 0.0).astype(BF)
        pairs_d = dot(place.astype(BF), pick, ((1,), (1,)))
        perm[d] = pairs_d.astype(BF)
        shared = (pairs_d * (1.0 / times)).astype(BF)
        g_mine[d] = dot(basis[:, zone(d)], shared).astype(BF)
    g_sent = transfer(
        [(g_mine.at[d], g_all.at[d ^ 1], around[d]) for d in range(4)], g_all, gs.at[0], gr.at[0]
    )

    for d in (2, 3, 0, 1):
        zone_arrived(0, d)
        block = rhs[zone(d), :].astype(F32) + dot(perm[d], got0[d])
        r0[zone(d), :] = block
        xw[0, zone(d), :] = split(weight[zone(d), :] * block)

    def coarse_send(k, local):
        cl_mine[k] = local
        cl_all[k, s] = local
        return transfer(
            [(cl_mine.at[k], cl_all.at[k, s], t) for t in mates],
            cl_all.at[k, pl.ds(0, N_SUB - 1)], cs.at[k], cr.at[k],
        )

    def coarse_setup():
        arrived(*map_sent)
        total = map_mine[...]
        for k in range(1, N_SUB):
            total = total + map_all[k]
        at_all = lax.broadcasted_iota(jnp.int32, (NL, NR), 0)
        for i in range(4):
            hot[:, NR * i : NR * (i + 1)] = jnp.where(
                at_all == total[i : i + 1, :], 1.0, 0.0
            ).astype(BF)
        picks = dot(cinv[...], hot[...]).T
        picks = jnp.concatenate([picks, picks], axis=1)
        half = lax.broadcasted_iota(jnp.int32, (NC_ALL, NR), 1) // OWN_ROWS
        picks = jnp.where(half == lax.rem(s, 2), picks, 0.0).astype(BF)
        e_mine[...] = picks.reshape(N_SUB, NC, NR)
        e_all[s] = e_mine[s]
        return transfer(
            [
                (e_mine.at[lax.rem(s + k, N_SUB)], e_all.at[s], mates[k - 1])
                for k in range(1, N_SUB)
            ],
            e_all.at[pl.ds(0, N_SUB - 1)], es.at[0], er.at[0],
        )

    def coarse_finish(e_sent):
        arrived(*e_sent)
        picks = jnp.concatenate([e_all[2 * i] + e_all[2 * i + 1] for i in range(N_SUB // 2)], axis=1)
        coarse[...] = dot(picks, hot[...]).astype(BF)

    def local_apply(matrix, blocks, d):
        return fold(dot(matrix[zone(d), :], blocks))

    def local_part(k, e):
        blocks = xw[k]
        for d in range(4):
            ship(e, d, weight[zone(d), :] * local_apply(linv, blocks, d))

    def coarse_part(k, e, gathered):
        arrived(*gathered)
        terms = split(cl_all[k].reshape(NC_ALL, NR))
        values = fold(dot(coarse[...], terms))
        pk_mine[k] = values
        values_sent = transfer(
            [(pk_mine.at[k], pk_all.at[k, d ^ 1], around[d]) for d in range(4)],
            pk_all.at[k], ps.at[k], pr.at[k],
        )
        picked = split(values)
        for d in range(4):
            part = fold(dot(basis[:, zone(d)], picked, ((0,), (0,))))
            loc[zone(d), :] = sent[e - 1, zone(d), :] + weight[zone(d), :] * part
        return values_sent

    def finish_z(k, e, values_sent):
        arrived(*values_sent)
        steps_arrived(e)
        for d in (2, 3, 0, 1):
            theirs = fold(dot(g_all[d], split(pk_all[k, d]), ((0,), (0,))))
            mine = loc[zone(d), :] + theirs
            xz[k, zone(d), :] = split(mine + shipped(e, d))

    def shares_setup():
        row = lax.broadcasted_iota(jnp.int32, (ZONE, ZONE), 0)
        column = lax.broadcasted_iota(jnp.int32, (ZONE, ZONE), 1)
        own = jnp.zeros((NC, NL), F32)
        for d in range(4):
            both = jnp.concatenate([weight[zone(d), :], weight[zone(d), :]], axis=1)
            scaled = dot(basis[:, zone(d)], jnp.where(row == column, both, 0.0).astype(BF)).astype(BF)
            own = own + dot(scaled, schur[zone(d), :])
            put_rows(d, dot(g_all[d], schur[zone(d), :]))
        put_rows(4, own)

    def put_rows(i, rows_f):
        hi = rows_f.astype(BF)
        gs_rows[pl.ds(2 * NC * i, NC), :] = hi
        gs_rows[pl.ds(2 * NC * i + NC, NC), :] = (rows_f - hi.astype(F32)).astype(BF)

    def operate(k, e, coarse_too):
        blocks = xz[k]
        if coarse_too:
            terms = fold(dot(gs_rows[...], blocks))
            terms = [
                terms[2 * NC * i : 2 * NC * i + NC] + terms[2 * NC * i + NC : 2 * NC * (i + 1)]
                for i in range(5)
            ]
            for d in range(4):
                ct_mine[k, d] = terms[d]
                remote(ct_mine.at[k, d], ct_all.at[k, d ^ 1], ts.at[k], tr.at[k], around[d])
            started.append((ct_all.at[k], ts.at[k]))
            own_share[...] = terms[4]
        for d in range(4):
            ship(e, d, local_apply(schur, blocks, d))

    def coarse_shares(k, e):
        total = own_share[...]
        arrived(ct_all.at[k], tr.at[k])
        for d in range(4):
            total = total + ct_all[k, d]
        return coarse_send(k + 1, total)

    def finish_q(k, e):
        steps_arrived(e)
        for d in (2, 3, 0, 1):
            whole = sent[e - 1, zone(d), :] + shipped(e, d)
            xw[k + 1, zone(d), :] = split(weight[zone(d), :] * whole)

    def reduce_start(i):
        share = AR_ROWS[i] // N_GROUP

        def part(t):
            return pl.ds(pl.multiple_of(share * t, 8), share)

        ar_r1[i][g] = ar_in[i][part(g), :]
        return transfer(
            [(ar_in[i].at[part(t[0])], ar_r1[i].at[g], t) for t in peers],
            ar_r1[i].at[pl.ds(0, N_GROUP - 1)], as1.at[i], ar1.at[i],
        )

    def reduce_spread(i, step, total, targets, send_sem, recv_sem):
        ar_p[i][step] = total
        slot = (s, lax.rem(s, 4), lax.div(s, 4))[step]
        ar_r2[i][step, slot] = total
        return transfer(
            [(ar_p[i].at[step], ar_r2[i].at[step, slot], t) for t in targets],
            ar_r2[i].at[step, pl.ds(0, len(targets))], send_sem.at[i], recv_sem.at[i],
        )

    def reduce_sum(i, step, waits, count):
        arrived(*waits)
        total = ar_r2[i][step, 0]
        for k in range(1, count):
            total = total + ar_r2[i][step, k]
        return total

    def reduce_middle(i, waits):
        arrived(*waits)
        total = ar_r1[i][0]
        for k in range(1, N_GROUP):
            total = total + ar_r1[i][k]
        if i == 3:
            return reduce_spread(i, 0, total, mates, as2, ar2)
        return reduce_spread(i, 1, total, mates_y, as2, ar2)

    def reduce_more(i, waits):
        return reduce_spread(i, 2, reduce_sum(i, 1, waits, 4), mates_z, as4, ar4)

    def reduce_last(i, waits):
        share = AR_ROWS[i] // N_GROUP
        total = reduce_sum(i, 0, waits, N_SUB) if i == 3 else reduce_sum(i, 2, waits, 4)
        ar_q[i][...] = total
        mine = pl.ds(pl.multiple_of(share * g, 8), share)
        ar_out[i][mine, :] = total
        return transfer(
            [(ar_q[i], ar_out[i].at[mine], t) for t in peers],
            ar_out[i].at[pl.ds(0, share * (N_GROUP - 1))], as3.at[i], ar3.at[i],
        )

    def reduce_wait(waits):
        arrived(*waits)

    gathered = coarse_send(0, fold(dot(basis[...], xw[0])))
    e_sent = coarse_setup()
    load_l.wait()
    local_part(0, 1)
    arrived(*g_sent)
    load_s.wait()
    shares_setup()
    coarse_finish(e_sent)
    values_sent = coarse_part(0, 1, gathered)
    finish_z(0, 1, values_sent)

    operate(0, 2, True)
    gathered = coarse_shares(0, 2)
    ar_in[0][0:NR, :] = gram(xz[0], xw[0])
    finish_q(0, 2)
    local_part(1, 3)
    ar_in[0][NR:, :] = gram(xz[0], xw[1])
    ar_a = reduce_start(0)
    values_sent = coarse_part(1, 3, gathered)
    ar_a = reduce_middle(0, ar_a)
    finish_z(1, 3, values_sent)

    operate(1, 4, True)
    ar_a = reduce_more(0, ar_a)
    gathered = coarse_shares(1, 4)
    ar_in[1][0:NR, :] = gram(xz[1], xw[1])
    ar_a = reduce_last(0, ar_a)
    finish_q(1, 4)
    local_part(2, 5)
    ar_in[1][NR:, :] = gram(xz[1], xw[2])
    ar_b = reduce_start(1)
    reduce_wait(ar_a)
    mat[0] = sym(ar_out[0][NR:, :])
    invert_lead(top.at[0], mat.at[0])
    invert_steps(top.at[0], 0, 32)
    values_sent = coarse_part(2, 5, gathered)
    ar_b = reduce_middle(1, ar_b)
    invert_steps(top.at[0], 32, 64)
    invert_next(top.at[0], bottom.at[0], mat.at[0])
    finish_z(2, 5, values_sent)

    operate(2, 6, False)
    ar_in[2][...] = gram(xz[2], xw[2])
    ar_c = reduce_start(2)
    ar_b = reduce_more(1, ar_b)
    invert_steps(bottom.at[0], 0, 64)
    inv1 = invert_end(top.at[0], bottom.at[0])
    m0 = ar_out[0][0:NR, :]
    ar_b = reduce_last(1, ar_b)
    t0 = small(inv1, m0)
    finish_q(2, 6)
    ar_in[3][...] = gram(xz[2], xw[3])
    ar_d = reduce_start(3)
    ar_c = reduce_middle(2, ar_c)
    reduce_wait(ar_b)
    m2 = sym(ar_out[1][0:NR, :])
    m3 = sym(ar_out[1][NR:, :])
    t2 = small(inv1, m2)
    mat[1] = sym(m3 - small(m2, t2))
    invert_lead(top.at[1], mat.at[1])
    ar_d = reduce_middle(3, ar_d)
    ar_c = reduce_more(2, ar_c)
    invert_steps(top.at[1], 0, 64)
    invert_next(top.at[1], bottom.at[1], mat.at[1])
    ar_c = reduce_last(2, ar_c)
    invert_steps(bottom.at[1], 0, 32)
    ar_d = reduce_last(3, ar_d)
    invert_steps(bottom.at[1], 32, 64)
    inv2 = invert_end(top.at[1], bottom.at[1])
    t3 = small(inv1, m3)
    h1 = mat[0] - small(m2, t0)
    reduce_wait(ar_c)
    m4 = sym(ar_out[2][...])
    s23 = m4 - small(m2, t3)
    y = small(inv2, s23)
    u1 = small(inv2, h1)
    h2 = m2 - small(m3, t0) - small_t(s23, u1)
    part = small(m3, t3) + small_t(s23, y)
    a0 = t0 - small(t2, u1)
    d0 = small(t2, y) - t3
    x_out[...] = combine(xz[0], a0) + combine(xz[1], u1)
    xd = xz[2]
    base[0] = split(
        xd[:, :NR].astype(F32) + xd[:, NR:].astype(F32) - combine(xz[1], y) + combine(xz[0], d0)
    )
    r_out[...] = r0[...] - mult[...] * (combine(xw[1], a0) + combine(xw[2], u1))
    qd = xw[3]
    base[1] = split(
        qd[:, :NR].astype(F32) + qd[:, NR:].astype(F32) - combine(xw[2], y) + combine(xw[1], d0)
    )
    reduce_wait(ar_d)
    mat[2] = sym(ar_out[3][...] - part)
    invert_lead(top.at[2], mat.at[2])
    invert_steps(top.at[2], 0, 64)
    invert_next(top.at[2], bottom.at[2], mat.at[2])
    cross = top[2, :, HALF:]
    above = small(top[2, :, :HALF], h2[:HALF])
    below = h2[HALF:] - small_t(cross, h2[:HALF])
    invert_steps(bottom.at[2], 0, 64)
    below = small(bottom[2, :, :HALF], below)
    c2 = jnp.concatenate([above - small(cross, below), below], axis=0)
    x_out[...] = x_out[...] + combine(base[0], c2)
    r_out[...] = r_out[...] - mult[...] * combine(base[1], c2)
    for span, sem in started:
        arrived(span, sem)


def shards(
    schur, local_inverse, rhs_parts, basis, coarse_map, coarse_inverse, shared_rows, shared_counts
):
    vmem = pl.BlockSpec(memory_space=pltpu.VMEM)
    in_hbm = pl.BlockSpec(memory_space=pltpu.HBM)
    dma = pltpu.SemaphoreType.DMA
    ar_shapes = [r // N_GROUP for r in AR_ROWS]
    scratch = [
        pltpu.VMEM((NL, NL), BF),
        pltpu.VMEM((NL, NL), BF),
        pltpu.VMEM((NL, NR), BF),
        pltpu.VMEM((NC, NL), BF),
        pltpu.VMEM((1, NC), jnp.int32),
        pltpu.VMEM((OWN_ROWS, NL), BF),
        pltpu.VMEM((2, 4, ZONE), jnp.int32),
        pltpu.VMEM((1, 4), jnp.int32),
        pltpu.VMEM((4, ZONE, ZONE), BF),
        pltpu.VMEM((NL, NR), F32),
        pltpu.VMEM((NL, NR), F32),
        pltpu.VMEM((6, NL, NR), F32),
        pltpu.VMEM((6, NL, NR), jnp.int16),
        pltpu.VMEM((6, 4, 8, NR), F32),
        pltpu.VMEM((6, 4, 8, NR), F32),
        pltpu.VMEM((4, ZONE, NR), BF),
        pltpu.VMEM((6, 4, ZONE, NR), jnp.int16),
        pltpu.VMEM((NL, NR), F32),
        pltpu.VMEM((4, NL, 2 * NR), BF),
        pltpu.VMEM((3, NL, 2 * NR), BF),
        pltpu.VMEM((NL, NR), F32),
        pltpu.VMEM((2, NL, 2 * NR), BF),
        pltpu.VMEM((3, NC, NR), F32),
        pltpu.VMEM((3, N_SUB, NC, NR), F32),
        pltpu.VMEM((8, NR), jnp.int32),
        pltpu.VMEM((N_SUB, 8, NR), jnp.int32),
        pltpu.VMEM((NL, NC_ALL), BF),
        pltpu.VMEM((N_SUB, NC, NR), BF),
        pltpu.VMEM((N_SUB, NC, NR), BF),
        pltpu.VMEM((NC, NC_ALL), BF),
        pltpu.VMEM((3, NR, NR), F32),
        pltpu.VMEM((3, HALF, NR), F32),
        pltpu.VMEM((3, HALF, NR), F32),
        pltpu.VMEM((4, NC, ZONE), BF),
        pltpu.VMEM((4, NC, ZONE), BF),
        pltpu.VMEM((2, 4, NC, NR), F32),
        pltpu.VMEM((2, 4, NC, NR), F32),
        pltpu.VMEM((10 * NC, NL), BF),
        pltpu.VMEM((NC, NR), F32),
        pltpu.VMEM((3, NC, NR), F32),
        pltpu.VMEM((3, 4, NC, NR), F32),
        [pltpu.VMEM((r, NR), F32) for r in AR_ROWS],
        [pltpu.VMEM((N_GROUP, r, NR), F32) for r in ar_shapes],
        [pltpu.VMEM((3, r, NR), F32) for r in ar_shapes],
        [pltpu.VMEM((3, N_SUB, r, NR), F32) for r in ar_shapes],
        [pltpu.VMEM((r, NR), F32) for r in ar_shapes],
        [pltpu.VMEM((r, NR), F32) for r in AR_ROWS],
        dma((8,)),
        dma((7,)),
        dma((7, 4)),
        dma((3,)),
        dma((3,)),
        dma((1,)),
        dma((1,)),
        dma((1,)),
        dma((1,)),
        dma((4,)),
        dma((4,)),
        dma((4,)),
        dma((4,)),
        dma((4,)),
        dma((4,)),
        dma((4,)),
        dma((4,)),
        dma((1,)),
        dma((1,)),
        dma((2,)),
        dma((2,)),
        dma((3,)),
        dma((3,)),
        dma((6,)),
        dma((6,)),
    ]
    out = jax.ShapeDtypeStruct((NL, NR), F32)
    x, r = pl.pallas_call(
        kernel,
        out_shape=(out, out),
        in_specs=[in_hbm] * 8,
        out_specs=(vmem, vmem),
        scratch_shapes=scratch,
        compiler_params=pltpu.CompilerParams(
            collective_id=0, has_side_effects=True, vmem_limit_bytes=40 * 1024 * 1024
        ),
        name="block_cg",
    )(
        *[
            pltpu.with_memory_space_constraint(a, pltpu.HBM)
            for a in (
                schur[0, 0], local_inverse[0, 0], rhs_parts[0, 0], basis[0, 0], coarse_map[0],
                coarse_inverse[0], shared_rows[0, 0], shared_counts[0],
            )
        ]
    )
    return x[None, None], r[None, None]


def solution(mesh):
    placed = (
        P("group", "sub", None, None),
        P("group", "sub", None, None),
        P("group", "sub", None, None),
        P("group", "sub", None, None),
        P("group", "sub", None),
        P("group", "sub", None),
        P("group", "sub", None, None, None),
        P("group", "sub", None),
    )
    return jax.shard_map(
        shards,
        mesh=mesh,
        in_specs=placed,
        out_specs=(P("group", "sub", None, None), P("group", "sub", None, None)),
        check_vma=False,
    )
```

```python
import functools

import jax
import jax.numpy as jnp
from jax import lax
from jax.experimental import pallas as pl
from jax.experimental.pallas import tpu as pltpu
from jax.sharding import PartitionSpec as P

BF = jnp.bfloat16
F32 = jnp.float32
MESH = pl.DeviceIdType.MESH
N_GROUP = 8
N_SUB = 16
NL = 1024
ZONE = 256
NR = 128
NC = 32
NC_ALL = NC * N_SUB
OWN_ROWS = 64
HALF = NR // 2
AR_ROWS = (256, 256, 128, 128)


def split(x):
    hi = x.astype(BF)
    lo = (x - hi.astype(F32)).astype(BF)
    return jnp.concatenate([hi, lo], axis=-1)


def fold(y):
    return y[:, :NR] + y[:, NR:]


def dot(a, b, dims=((1,), (0,))):
    return lax.dot_general(a, b, (dims, ((), ())), preferred_element_type=F32)


def small(a, b):
    return jnp.dot(a, b, precision=lax.Precision.HIGHEST, preferred_element_type=F32)


def gram(left, right):
    full = dot(left, right, ((0,), (0,)))
    half = full[:NR] + full[NR:]
    return half[:, :NR] + half[:, NR:]


def sym(a):
    return 0.5 * (a + a.T)


def combine(blocks, mixing):
    halves = split(mixing)
    return fold(dot(blocks, jnp.concatenate([halves, halves], axis=0)))


def invert_steps(mat, first, last):
    lane = lax.broadcasted_iota(jnp.int32, (HALF, NR), 1)
    sub = lax.broadcasted_iota(jnp.int32, (HALF, NR), 0)
    lane8 = lax.broadcasted_iota(jnp.int32, (8, NR), 1)

    def column(a, lanes, j):
        return jnp.broadcast_to(
            jnp.sum(jnp.where(lanes == j, a, 0.0), axis=1, keepdims=True), a.shape
        )

    def step(i, carry):
        k = 4 * i
        a = mat[...]
        r = [jnp.broadcast_to(mat[pl.ds(k + j, 1), :], (8, NR)) for j in range(4)]
        c = [column(a, lane, k + j) for j in range(4)]
        d = [[column(r[m], lane8, k + j) for j in range(4)] for m in range(4)]
        inside = (lane8 >= k) & (lane8 < k + 4)
        q = [jnp.where(lane8 == k + j, 1.0, jnp.where(inside, 0.0, r[j])) for j in range(4)]
        i0 = 1.0 / (d[0][0] * d[1][1] - d[0][1] * d[1][0])

        def lead(x0, x1):
            return (d[1][1] * x0 - d[0][1] * x1) * i0, (d[0][0] * x1 - d[1][0] * x0) * i0

        e02, e12 = lead(d[0][2], d[1][2])
        e03, e13 = lead(d[0][3], d[1][3])
        f0, f1 = lead(q[0], q[1])
        s22 = d[2][2] - d[2][0] * e02 - d[2][1] * e12
        s23 = d[2][3] - d[2][0] * e03 - d[2][1] * e13
        s32 = d[3][2] - d[3][0] * e02 - d[3][1] * e12
        s33 = d[3][3] - d[3][0] * e03 - d[3][1] * e13
        g2 = q[2] - d[2][0] * f0 - d[2][1] * f1
        g3 = q[3] - d[3][0] * f0 - d[3][1] * f1
        i1 = 1.0 / (s22 * s33 - s23 * s32)
        w2 = (s33 * g2 - s23 * g3) * i1
        w3 = (s22 * g3 - s32 * g2) * i1
        w = [f0 - e02 * w2 - e03 * w3, f1 - e12 * w2 - e13 * w3, w2, w3]
        w = [x[0:1] for x in w]
        new = jnp.where((lane >= k) & (lane < k + 4), 0.0, a)
        new = new - (c[0] * w[0] + c[1] * w[1]) - (c[2] * w[2] + c[3] * w[3])
        for j in range(4):
            new = jnp.where(sub == k + j, w[j], new)
        mat[...] = new
        return carry

    lax.fori_loop(first // 4, last // 4, step, 0)


def small_t(a, b):
    return lax.dot_general(
        a, b, (((0,), (0,)), ((), ())), precision=lax.Precision.HIGHEST, preferred_element_type=F32
    )


def invert_lead(top, mat):
    top[...] = mat[0:HALF, :]


def invert_next(top, bottom, mat):
    rest = mat[HALF:, HALF:] - small_t(mat[0:HALF, HALF:], top[:, HALF:])
    bottom[...] = jnp.concatenate([rest, jnp.zeros((HALF, HALF), F32)], axis=1)


def invert_end(top, bottom):
    x = top[:, HALF:]
    low = bottom[:, :HALF]
    xl = small(x, low)
    corner = top[:, :HALF] + lax.dot_general(
        xl, x, (((1,), (1,)), ((), ())), precision=lax.Precision.HIGHEST, preferred_element_type=F32
    )
    upper = jnp.concatenate([corner, -xl], axis=1)
    lower = jnp.concatenate([-xl.T, low], axis=1)
    return jnp.concatenate([upper, lower], axis=0)


def kernel(
    schur_h, linv_h, rhs_h, basis_h, cmap_h, cinv_h, rows_h, counts_h,
    x_out, r_out,
    schur, linv, rhs, basis, cmap, cinv, rows, counts, perm, weight, mult, sent, coded, step_mine, step_all, got0, got, r0, xw, xz, loc,
    cl_mine, cl_all, map_mine, map_all, hot, e_mine, e_all, coarse, mat, top, bottom, g_mine, g_all, ct_mine, ct_all, gs_rows, own_share, pk_mine, pk_all,
    ar_in, ar_r1, ar_p, ar_r2, ar_q, ar_out,
    load_sem, xs, xr, cs, cr, ms, mr, es, er, as1, ar1, as2, ar2, as3, ar3, as4, ar4, gs, gr, ts, tr, ps, pr, qs, qr,
):
    g = lax.axis_index("group")
    s = lax.axis_index("sub")
    started = []

    def remote(src, dst, send_sem, recv_sem, target):
        copy = pltpu.make_async_remote_copy(
            src_ref=src, dst_ref=dst, send_sem=send_sem, recv_sem=recv_sem,
            device_id=target, device_id_type=MESH,
        )
        copy.start()

    def arrived(span, sem):
        pltpu.make_async_copy(span, span, sem).wait()

    def transfer(copies, span, send_sem, recv_sem):
        for src, dst, target in copies:
            remote(src, dst, send_sem, recv_sem, target)
        started.append((span, send_sem))
        return span, recv_sem

    pairs = (
        (cmap_h, cmap), (rhs_h, rhs), (rows_h, rows), (counts_h, counts),
        (basis_h, basis), (cinv_h, cinv), (linv_h, linv), (schur_h, schur),
    )
    loads = [pltpu.make_async_copy(a, b, load_sem.at[i]) for i, (a, b) in enumerate(pairs)]
    for load in loads:
        load.start()
    load_l, load_s = loads[6:]

    barrier = pltpu.get_barrier_semaphore()
    mates = [(g, lax.rem(s + k, N_SUB)) for k in range(1, N_SUB)]
    peers = [(lax.rem(g + k, N_GROUP), s) for k in range(1, N_GROUP)]
    y, z = lax.rem(s, 4), lax.div(s, 4)
    mates_y = [(g, 4 * z + lax.rem(y + k, 4)) for k in range(1, 4)]
    mates_z = [(g, 4 * lax.rem(z + k, 4) + y) for k in range(1, 4)]
    for target in mates + peers:
        pl.semaphore_signal(barrier, inc=1, device_id=target, device_id_type=MESH)

    map_mine[...] = jnp.zeros((8, NR), jnp.int32)
    loads[0].wait()
    map_mine[0:1, 0:NC] = cmap[...]
    tile = jnp.broadcast_to(map_mine[0:1, :], (8, NR))
    tile = pltpu.roll(tile, NC * lax.rem(s, 4), 1)
    at_row = lax.broadcasted_iota(jnp.int32, (8, NR), 0) == lax.div(s, 4)
    map_mine[...] = jnp.where(at_row, tile, 0)

    for load in loads[1:6]:
        load.wait()
    pl.semaphore_wait(barrier, len(mates) + len(peers))

    around = [
        (g, lax.rem(s + 1, N_SUB)),
        (g, lax.rem(s + N_SUB - 1, N_SUB)),
        (lax.rem(g + 1, N_GROUP), s),
        (lax.rem(g + N_GROUP - 1, N_GROUP), s),
    ]

    def send_zone(e, d, src, dst):
        remote(src, dst.at[d ^ 1], xs.at[e], xr.at[e, d ^ 1], around[d])
        if d == 3:
            started.append((dst, xs.at[e]))

    def ship(e, d, value):
        sent[e - 1, zone(d), :] = value
        top_value = jnp.maximum(jnp.max(jnp.abs(value), axis=0, keepdims=True), 2e-34)
        step_mine[e - 1, d] = jnp.broadcast_to(top_value * (1.0 / 32767.0), (8, NR))
        remote(
            step_mine.at[e - 1, d], step_all.at[e - 1, d ^ 1], qs.at[e - 1], qr.at[e - 1], around[d]
        )
        if d == 3:
            started.append((step_all.at[e - 1], qs.at[e - 1]))
        steps = jnp.round(value * (32767.0 / top_value))
        coded[e - 1, zone(d), :] = steps.astype(jnp.int32).astype(jnp.int16)
        send_zone(e, d, coded.at[e - 1, zone(d)], got.at[e - 1])

    def steps_arrived(e):
        arrived(step_all.at[e - 1], qr.at[e - 1])

    def shipped(e, d):
        zone_arrived(e, d)
        steps = got[e - 1, d].astype(jnp.int32).astype(F32)
        return fold(dot(perm[d], split(steps))) * step_all[e - 1, d, 0:1, :]

    def zone_arrived(e, d):
        zones = got0 if e == 0 else got.at[e - 1]
        arrived(zones.at[d], xr.at[e, d])

    def zone(d):
        return pl.ds(ZONE * d, ZONE)

    for d in range(4):
        send_zone(0, d, rhs.at[zone(d)], got0)
    map_sent = transfer(
        [(map_mine, map_all.at[k], mates[k - 1]) for k in range(1, N_SUB)],
        map_all.at[pl.ds(0, N_SUB - 1)], ms.at[0], mr.at[0],
    )

    lane = lax.broadcasted_iota(jnp.int32, (1, ZONE), 1)
    at = lax.broadcasted_iota(jnp.int32, (ZONE, ZONE), 0)
    for d in range(4):
        mine = jnp.where(lane < counts[0:1, d : d + 1], rows[0, d : d + 1, :] - ZONE * d, -1)
        theirs = rows[1, d : d + 1, :] - ZONE * (d ^ 1)
        place = jnp.where(at == mine, 1.0, 0.0)
        times = 1.0 + jnp.sum(place, axis=1, keepdims=True)
        mult[zone(d), :] = jnp.broadcast_to(times, (ZONE, NR))
        weight[zone(d), :] = jnp.broadcast_to(1.0 / times, (ZONE, NR))
        pick = jnp.where(at == theirs, 1.0, 0.0).astype(BF)
        pairs_d = dot(place.astype(BF), pick, ((1,), (1,)))
        perm[d] = pairs_d.astype(BF)
        shared = (pairs_d * (1.0 / times)).astype(BF)
        g_mine[d] = dot(basis[:, zone(d)], shared).astype(BF)
    g_sent = transfer(
        [(g_mine.at[d], g_all.at[d ^ 1], around[d]) for d in range(4)], g_all, gs.at[0], gr.at[0]
    )

    for d in (2, 3, 0, 1):
        zone_arrived(0, d)
        block = rhs[zone(d), :].astype(F32) + dot(perm[d], got0[d])
        r0[zone(d), :] = block
        xw[0, zone(d), :] = split(weight[zone(d), :] * block)

    def coarse_send(k, local):
        cl_mine[k] = local
        cl_all[k, s] = local
        return transfer(
            [(cl_mine.at[k], cl_all.at[k, s], t) for t in mates],
            cl_all.at[k, pl.ds(0, N_SUB - 1)], cs.at[k], cr.at[k],
        )

    def coarse_setup():
        arrived(*map_sent)
        total = map_mine[...]
        for k in range(1, N_SUB):
            total = total + map_all[k]
        at_all = lax.broadcasted_iota(jnp.int32, (NL, NR), 0)
        for i in range(4):
            hot[:, NR * i : NR * (i + 1)] = jnp.where(
                at_all == total[i : i + 1, :], 1.0, 0.0
            ).astype(BF)
        picks = dot(cinv[...], hot[...]).T
        picks = jnp.concatenate([picks, picks], axis=1)
        half = lax.broadcasted_iota(jnp.int32, (NC_ALL, NR), 1) // OWN_ROWS
        picks = jnp.where(half == lax.rem(s, 2), picks, 0.0).astype(BF)
        e_mine[...] = picks.reshape(N_SUB, NC, NR)
        e_all[s] = e_mine[s]
        return transfer(
            [
                (e_mine.at[lax.rem(s + k, N_SUB)], e_all.at[s], mates[k - 1])
                for k in range(1, N_SUB)
            ],
            e_all.at[pl.ds(0, N_SUB - 1)], es.at[0], er.at[0],
        )

    def coarse_finish(e_sent):
        arrived(*e_sent)
        picks = jnp.concatenate([e_all[2 * i] + e_all[2 * i + 1] for i in range(N_SUB // 2)], axis=1)
        coarse[...] = dot(picks, hot[...]).astype(BF)

    def local_apply(matrix, blocks, d):
        return fold(dot(matrix[zone(d), :], blocks))

    def local_part(k, e):
        blocks = xw[k]
        for d in range(4):
            ship(e, d, weight[zone(d), :] * local_apply(linv, blocks, d))

    def coarse_part(k, e, gathered):
        arrived(*gathered)
        terms = split(cl_all[k].reshape(NC_ALL, NR))
        values = fold(dot(coarse[...], terms))
        pk_mine[k] = values
        values_sent = transfer(
            [(pk_mine.at[k], pk_all.at[k, d ^ 1], around[d]) for d in range(4)],
            pk_all.at[k], ps.at[k], pr.at[k],
        )
        picked = split(values)
        for d in range(4):
            part = fold(dot(basis[:, zone(d)], picked, ((0,), (0,))))
            loc[zone(d), :] = sent[e - 1, zone(d), :] + weight[zone(d), :] * part
        return values_sent

    def finish_z(k, e, values_sent):
        arrived(*values_sent)
        steps_arrived(e)
        for d in (2, 3, 0, 1):
            theirs = fold(dot(g_all[d], split(pk_all[k, d]), ((0,), (0,))))
            mine = loc[zone(d), :] + theirs
            xz[k, zone(d), :] = split(mine + shipped(e, d))

    def shares_setup():
        row = lax.broadcasted_iota(jnp.int32, (ZONE, ZONE), 0)
        column = lax.broadcasted_iota(jnp.int32, (ZONE, ZONE), 1)
        own = jnp.zeros((NC, NL), F32)
        for d in range(4):
            both = jnp.concatenate([weight[zone(d), :], weight[zone(d), :]], axis=1)
            scaled = dot(basis[:, zone(d)], jnp.where(row == column, both, 0.0).astype(BF)).astype(BF)
            own = own + dot(scaled, schur[zone(d), :])
            put_rows(d, dot(g_all[d], schur[zone(d), :]))
        put_rows(4, own)

    def put_rows(i, rows_f):
        hi = rows_f.astype(BF)
        gs_rows[pl.ds(2 * NC * i, NC), :] = hi
        gs_rows[pl.ds(2 * NC * i + NC, NC), :] = (rows_f - hi.astype(F32)).astype(BF)

    def operate(k, e, coarse_too):
        blocks = xz[k]
        if coarse_too:
            terms = fold(dot(gs_rows[...], blocks))
            terms = [
                terms[2 * NC * i : 2 * NC * i + NC] + terms[2 * NC * i + NC : 2 * NC * (i + 1)]
                for i in range(5)
            ]
            for d in range(4):
                ct_mine[k, d] = terms[d]
                remote(ct_mine.at[k, d], ct_all.at[k, d ^ 1], ts.at[k], tr.at[k], around[d])
            started.append((ct_all.at[k], ts.at[k]))
            own_share[...] = terms[4]
        for d in range(4):
            ship(e, d, local_apply(schur, blocks, d))

    def coarse_shares(k, e):
        total = own_share[...]
        arrived(ct_all.at[k], tr.at[k])
        for d in range(4):
            total = total + ct_all[k, d]
        return coarse_send(k + 1, total)

    def finish_q(k, e):
        steps_arrived(e)
        for d in (2, 3, 0, 1):
            whole = sent[e - 1, zone(d), :] + shipped(e, d)
            xw[k + 1, zone(d), :] = split(weight[zone(d), :] * whole)

    def reduce_start(i):
        share = AR_ROWS[i] // N_GROUP

        def part(t):
            return pl.ds(pl.multiple_of(share * t, 8), share)

        ar_r1[i][g] = ar_in[i][part(g), :]
        return transfer(
            [(ar_in[i].at[part(t[0])], ar_r1[i].at[g], t) for t in peers],
            ar_r1[i].at[pl.ds(0, N_GROUP - 1)], as1.at[i], ar1.at[i],
        )

    def reduce_spread(i, step, total, targets, send_sem, recv_sem):
        ar_p[i][step] = total
        slot = (s, lax.rem(s, 4), lax.div(s, 4))[step]
        ar_r2[i][step, slot] = total
        return transfer(
            [(ar_p[i].at[step], ar_r2[i].at[step, slot], t) for t in targets],
            ar_r2[i].at[step, pl.ds(0, len(targets))], send_sem.at[i], recv_sem.at[i],
        )

    def reduce_sum(i, step, waits, count):
        arrived(*waits)
        total = ar_r2[i][step, 0]
        for k in range(1, count):
            total = total + ar_r2[i][step, k]
        return total

    def reduce_middle(i, waits):
        arrived(*waits)
        total = ar_r1[i][0]
        for k in range(1, N_GROUP):
            total = total + ar_r1[i][k]
        if i in (1, 2, 3):
            return reduce_spread(i, 0, total, mates, as2, ar2)
        return reduce_spread(i, 1, total, mates_y, as2, ar2)

    def reduce_more(i, waits):
        return reduce_spread(i, 2, reduce_sum(i, 1, waits, 4), mates_z, as4, ar4)

    def reduce_last(i, waits):
        share = AR_ROWS[i] // N_GROUP
        total = reduce_sum(i, 0, waits, N_SUB) if i in (1, 2, 3) else reduce_sum(i, 2, waits, 4)
        ar_q[i][...] = total
        mine = pl.ds(pl.multiple_of(share * g, 8), share)
        ar_out[i][mine, :] = total
        return transfer(
            [(ar_q[i], ar_out[i].at[mine], t) for t in peers],
            ar_out[i].at[pl.ds(0, share * (N_GROUP - 1))], as3.at[i], ar3.at[i],
        )

    def reduce_wait(waits):
        arrived(*waits)

    gathered = coarse_send(0, fold(dot(basis[...], xw[0])))
    e_sent = coarse_setup()
    load_l.wait()
    local_part(0, 1)
    arrived(*g_sent)
    load_s.wait()
    shares_setup()
    coarse_finish(e_sent)
    values_sent = coarse_part(0, 1, gathered)
    finish_z(0, 1, values_sent)

    operate(0, 2, True)
    gathered = coarse_shares(0, 2)
    ar_in[0][0:NR, :] = gram(xz[0], xw[0])
    finish_q(0, 2)
    local_part(1, 3)
    ar_in[0][NR:, :] = gram(xz[0], xw[1])
    ar_a = reduce_start(0)
    values_sent = coarse_part(1, 3, gathered)
    ar_a = reduce_middle(0, ar_a)
    finish_z(1, 3, values_sent)

    operate(1, 4, True)
    ar_a = reduce_more(0, ar_a)
    gathered = coarse_shares(1, 4)
    ar_in[1][0:NR, :] = gram(xz[1], xw[1])
    ar_a = reduce_last(0, ar_a)
    finish_q(1, 4)
    local_part(2, 5)
    ar_in[1][NR:, :] = gram(xz[1], xw[2])
    ar_b = reduce_start(1)
    values_sent = coarse_part(2, 5, gathered)
    reduce_wait(ar_a)
    mat[0] = sym(ar_out[0][NR:, :])
    invert_lead(top.at[0], mat.at[0])
    ar_b = reduce_middle(1, ar_b)
    finish_z(2, 5, values_sent)

    operate(2, 6, False)
    ar_in[2][...] = gram(xz[2], xw[2])
    ar_c = reduce_start(2)
    invert_steps(top.at[0], 0, 64)
    invert_next(top.at[0], bottom.at[0], mat.at[0])
    ar_b = reduce_last(1, ar_b)
    finish_q(2, 6)
    ar_in[3][...] = gram(xz[2], xw[3])
    ar_d = reduce_start(3)
    ar_c = reduce_middle(2, ar_c)
    invert_steps(bottom.at[0], 0, 64)
    inv1 = invert_end(top.at[0], bottom.at[0])
    m0 = ar_out[0][0:NR, :]
    t0 = small(inv1, m0)
    reduce_wait(ar_b)
    m2 = sym(ar_out[1][0:NR, :])
    m3 = sym(ar_out[1][NR:, :])
    t2 = small(inv1, m2)
    mat[1] = sym(m3 - small(m2, t2))
    invert_lead(top.at[1], mat.at[1])
    ar_d = reduce_middle(3, ar_d)
    invert_steps(top.at[1], 0, 64)
    invert_next(top.at[1], bottom.at[1], mat.at[1])
    ar_c = reduce_last(2, ar_c)
    invert_steps(bottom.at[1], 0, 32)
    ar_d = reduce_last(3, ar_d)
    invert_steps(bottom.at[1], 32, 64)
    inv2 = invert_end(top.at[1], bottom.at[1])
    t3 = small(inv1, m3)
    h1 = mat[0] - small(m2, t0)
    reduce_wait(ar_c)
    m4 = sym(ar_out[2][...])
    s23 = m4 - small(m2, t3)
    y = small(inv2, s23)
    u1 = small(inv2, h1)
    h2 = m2 - small(m3, t0) - small_t(s23, u1)
    part = small(m3, t3) + small_t(s23, y)
    a0 = t0 - small(t2, u1)
    d0 = small(t2, y) - t3
    reduce_wait(ar_d)
    mat[2] = sym(ar_out[3][...] - part)
    invert_lead(top.at[2], mat.at[2])
    invert_steps(top.at[2], 0, 64)
    invert_next(top.at[2], bottom.at[2], mat.at[2])
    cross = top[2, :, HALF:]
    above = small(top[2, :, :HALF], h2[:HALF])
    below = h2[HALF:] - small_t(cross, h2[:HALF])
    invert_steps(bottom.at[2], 0, 64)
    below = small(bottom[2, :, :HALF], below)
    c2 = jnp.concatenate([above - small(cross, below), below], axis=0)
    c1 = u1 - small(y, c2)
    c0 = a0 + small(d0, c2)
    x_out[...] = combine(xz[0], c0) + combine(xz[1], c1) + combine(xz[2], c2)
    r_out[...] = r0[...] - mult[...] * (combine(xw[1], c0) + combine(xw[2], c1) + combine(xw[3], c2))
    for span, sem in started:
        arrived(span, sem)


def shards(
    schur, local_inverse, rhs_parts, basis, coarse_map, coarse_inverse, shared_rows, shared_counts
):
    vmem = pl.BlockSpec(memory_space=pltpu.VMEM)
    in_hbm = pl.BlockSpec(memory_space=pltpu.HBM)
    dma = pltpu.SemaphoreType.DMA
    ar_shapes = [r // N_GROUP for r in AR_ROWS]
    scratch = [
        pltpu.VMEM((NL, NL), BF),
        pltpu.VMEM((NL, NL), BF),
        pltpu.VMEM((NL, NR), BF),
        pltpu.VMEM((NC, NL), BF),
        pltpu.VMEM((1, NC), jnp.int32),
        pltpu.VMEM((OWN_ROWS, NL), BF),
        pltpu.VMEM((2, 4, ZONE), jnp.int32),
        pltpu.VMEM((1, 4), jnp.int32),
        pltpu.VMEM((4, ZONE, ZONE), BF),
        pltpu.VMEM((NL, NR), F32),
        pltpu.VMEM((NL, NR), F32),
        pltpu.VMEM((6, NL, NR), F32),
        pltpu.VMEM((6, NL, NR), jnp.int16),
        pltpu.VMEM((6, 4, 8, NR), F32),
        pltpu.VMEM((6, 4, 8, NR), F32),
        pltpu.VMEM((4, ZONE, NR), BF),
        pltpu.VMEM((6, 4, ZONE, NR), jnp.int16),
        pltpu.VMEM((NL, NR), F32),
        pltpu.VMEM((4, NL, 2 * NR), BF),
        pltpu.VMEM((3, NL, 2 * NR), BF),
        pltpu.VMEM((NL, NR), F32),
        pltpu.VMEM((3, NC, NR), F32),
        pltpu.VMEM((3, N_SUB, NC, NR), F32),
        pltpu.VMEM((8, NR), jnp.int32),
        pltpu.VMEM((N_SUB, 8, NR), jnp.int32),
        pltpu.VMEM((NL, NC_ALL), BF),
        pltpu.VMEM((N_SUB, NC, NR), BF),
        pltpu.VMEM((N_SUB, NC, NR), BF),
        pltpu.VMEM((NC, NC_ALL), BF),
        pltpu.VMEM((3, NR, NR), F32),
        pltpu.VMEM((3, HALF, NR), F32),
        pltpu.VMEM((3, HALF, NR), F32),
        pltpu.VMEM((4, NC, ZONE), BF),
        pltpu.VMEM((4, NC, ZONE), BF),
        pltpu.VMEM((2, 4, NC, NR), F32),
        pltpu.VMEM((2, 4, NC, NR), F32),
        pltpu.VMEM((10 * NC, NL), BF),
        pltpu.VMEM((NC, NR), F32),
        pltpu.VMEM((3, NC, NR), F32),
        pltpu.VMEM((3, 4, NC, NR), F32),
        [pltpu.VMEM((r, NR), F32) for r in AR_ROWS],
        [pltpu.VMEM((N_GROUP, r, NR), F32) for r in ar_shapes],
        [pltpu.VMEM((3, r, NR), F32) for r in ar_shapes],
        [pltpu.VMEM((3, N_SUB, r, NR), F32) for r in ar_shapes],
        [pltpu.VMEM((r, NR), F32) for r in ar_shapes],
        [pltpu.VMEM((r, NR), F32) for r in AR_ROWS],
        dma((8,)),
        dma((7,)),
        dma((7, 4)),
        dma((3,)),
        dma((3,)),
        dma((1,)),
        dma((1,)),
        dma((1,)),
        dma((1,)),
        dma((4,)),
        dma((4,)),
        dma((4,)),
        dma((4,)),
        dma((4,)),
        dma((4,)),
        dma((4,)),
        dma((4,)),
        dma((1,)),
        dma((1,)),
        dma((2,)),
        dma((2,)),
        dma((3,)),
        dma((3,)),
        dma((6,)),
        dma((6,)),
    ]
    out = jax.ShapeDtypeStruct((NL, NR), F32)
    x, r = pl.pallas_call(
        kernel,
        out_shape=(out, out),
        in_specs=[in_hbm] * 8,
        out_specs=(vmem, vmem),
        scratch_shapes=scratch,
        compiler_params=pltpu.CompilerParams(
            collective_id=0, has_side_effects=True, vmem_limit_bytes=40 * 1024 * 1024
        ),
        name="block_cg",
    )(
        *[
            pltpu.with_memory_space_constraint(a, pltpu.HBM)
            for a in (
                schur[0, 0], local_inverse[0, 0], rhs_parts[0, 0], basis[0, 0], coarse_map[0],
                coarse_inverse[0], shared_rows[0, 0], shared_counts[0],
            )
        ]
    )
    return x[None, None], r[None, None]


def solution(mesh):
    placed = (
        P("group", "sub", None, None),
        P("group", "sub", None, None),
        P("group", "sub", None, None),
        P("group", "sub", None, None),
        P("group", "sub", None),
        P("group", "sub", None),
        P("group", "sub", None, None, None),
        P("group", "sub", None),
    )
    return jax.shard_map(
        shards,
        mesh=mesh,
        in_specs=placed,
        out_specs=(P("group", "sub", None, None), P("group", "sub", None, None)),
        check_vma=False,
    )
```

```python
import functools

import jax
import jax.numpy as jnp
from jax import lax
from jax.experimental import pallas as pl
from jax.experimental.pallas import tpu as pltpu
from jax.sharding import PartitionSpec as P

BF = jnp.bfloat16
F32 = jnp.float32
MESH = pl.DeviceIdType.MESH
N_GROUP = 8
N_SUB = 16
NL = 1024
ZONE = 256
NR = 128
NC = 32
NC_ALL = NC * N_SUB
OWN_ROWS = 64
HALF = NR // 2
AR_ROWS = (256, 256, 128, 128)


def split(x):
    hi = x.astype(BF)
    lo = (x - hi.astype(F32)).astype(BF)
    return jnp.concatenate([hi, lo], axis=-1)


def fold(y):
    return y[:, :NR] + y[:, NR:]


def dot(a, b, dims=((1,), (0,))):
    return lax.dot_general(a, b, (dims, ((), ())), preferred_element_type=F32)


def small(a, b):
    return jnp.dot(a, b, precision=lax.Precision.HIGHEST, preferred_element_type=F32)


def gram(left, right):
    full = dot(left, right, ((0,), (0,)))
    half = full[:NR] + full[NR:]
    return half[:, :NR] + half[:, NR:]


def sym(a):
    return 0.5 * (a + a.T)


def combine(blocks, mixing):
    halves = split(mixing)
    return fold(dot(blocks, jnp.concatenate([halves, halves], axis=0)))


def invert_steps(mat, first, last):
    lane = lax.broadcasted_iota(jnp.int32, (HALF, NR), 1)
    sub = lax.broadcasted_iota(jnp.int32, (HALF, NR), 0)
    lane8 = lax.broadcasted_iota(jnp.int32, (8, NR), 1)

    def column(a, lanes, j):
        return jnp.broadcast_to(
            jnp.sum(jnp.where(lanes == j, a, 0.0), axis=1, keepdims=True), a.shape
        )

    def step(i, carry):
        k = 4 * i
        a = mat[...]
        r = [jnp.broadcast_to(mat[pl.ds(k + j, 1), :], (8, NR)) for j in range(4)]
        c = [column(a, lane, k + j) for j in range(4)]
        d = [[column(r[m], lane8, k + j) for j in range(4)] for m in range(4)]
        inside = (lane8 >= k) & (lane8 < k + 4)
        q = [jnp.where(lane8 == k + j, 1.0, jnp.where(inside, 0.0, r[j])) for j in range(4)]
        i0 = 1.0 / (d[0][0] * d[1][1] - d[0][1] * d[1][0])

        def lead(x0, x1):
            return (d[1][1] * x0 - d[0][1] * x1) * i0, (d[0][0] * x1 - d[1][0] * x0) * i0

        e02, e12 = lead(d[0][2], d[1][2])
        e03, e13 = lead(d[0][3], d[1][3])
        f0, f1 = lead(q[0], q[1])
        s22 = d[2][2] - d[2][0] * e02 - d[2][1] * e12
        s23 = d[2][3] - d[2][0] * e03 - d[2][1] * e13
        s32 = d[3][2] - d[3][0] * e02 - d[3][1] * e12
        s33 = d[3][3] - d[3][0] * e03 - d[3][1] * e13
        g2 = q[2] - d[2][0] * f0 - d[2][1] * f1
        g3 = q[3] - d[3][0] * f0 - d[3][1] * f1
        i1 = 1.0 / (s22 * s33 - s23 * s32)
        w2 = (s33 * g2 - s23 * g3) * i1
        w3 = (s22 * g3 - s32 * g2) * i1
        w = [f0 - e02 * w2 - e03 * w3, f1 - e12 * w2 - e13 * w3, w2, w3]
        w = [x[0:1] for x in w]
        new = jnp.where((lane >= k) & (lane < k + 4), 0.0, a)
        new = new - (c[0] * w[0] + c[1] * w[1]) - (c[2] * w[2] + c[3] * w[3])
        for j in range(4):
            new = jnp.where(sub == k + j, w[j], new)
        mat[...] = new
        return carry

    lax.fori_loop(first // 4, last // 4, step, 0)


def small_t(a, b):
    return lax.dot_general(
        a, b, (((0,), (0,)), ((), ())), precision=lax.Precision.HIGHEST, preferred_element_type=F32
    )


def invert_lead(top, mat):
    top[...] = mat[0:HALF, :]


def invert_next(top, bottom, mat):
    rest = mat[HALF:, HALF:] - small_t(mat[0:HALF, HALF:], top[:, HALF:])
    bottom[...] = jnp.concatenate([rest, jnp.zeros((HALF, HALF), F32)], axis=1)


def invert_end(top, bottom):
    x = top[:, HALF:]
    low = bottom[:, :HALF]
    xl = small(x, low)
    corner = top[:, :HALF] + lax.dot_general(
        xl, x, (((1,), (1,)), ((), ())), precision=lax.Precision.HIGHEST, preferred_element_type=F32
    )
    upper = jnp.concatenate([corner, -xl], axis=1)
    lower = jnp.concatenate([-xl.T, low], axis=1)
    return jnp.concatenate([upper, lower], axis=0)


def kernel(
    schur_h, linv_h, rhs_h, basis_h, cmap_h, cinv_h, rows_h, counts_h,
    x_out, r_out,
    schur, linv, rhs, basis, cmap, cinv, rows, counts, perm, weight, mult, sent, coded, step_mine, step_all, got0, got, r0, xw, xz, loc,
    cl_mine, cl_all, map_mine, map_all, hot, e_mine, e_all, coarse, mat, top, bottom, g_mine, g_all, ct_mine, ct_all, gs_rows, own_share, pk_mine, pk_all,
    ar_in, ar_r1, ar_p, ar_r2, ar_q, ar_out,
    load_sem, xs, xr, cs, cr, ms, mr, es, er, as1, ar1, as2, ar2, as3, ar3, as4, ar4, gs, gr, ts, tr, ps, pr, qs, qr,
):
    g = lax.axis_index("group")
    s = lax.axis_index("sub")
    started = []

    def remote(src, dst, send_sem, recv_sem, target):
        copy = pltpu.make_async_remote_copy(
            src_ref=src, dst_ref=dst, send_sem=send_sem, recv_sem=recv_sem,
            device_id=target, device_id_type=MESH,
        )
        copy.start()

    def arrived(span, sem):
        pltpu.make_async_copy(span, span, sem).wait()

    def transfer(copies, span, send_sem, recv_sem):
        for src, dst, target in copies:
            remote(src, dst, send_sem, recv_sem, target)
        started.append((span, send_sem))
        return span, recv_sem

    pairs = (
        (cmap_h, cmap), (rhs_h, rhs), (rows_h, rows), (counts_h, counts),
        (basis_h, basis), (cinv_h, cinv), (linv_h, linv), (schur_h, schur),
    )
    loads = [pltpu.make_async_copy(a, b, load_sem.at[i]) for i, (a, b) in enumerate(pairs)]
    for load in loads:
        load.start()
    load_l, load_s = loads[6:]

    barrier = pltpu.get_barrier_semaphore()
    mates = [(g, lax.rem(s + k, N_SUB)) for k in range(1, N_SUB)]
    peers = [(lax.rem(g + k, N_GROUP), s) for k in range(1, N_GROUP)]
    y, z = lax.rem(s, 4), lax.div(s, 4)
    mates_y = [(g, 4 * z + lax.rem(y + k, 4)) for k in range(1, 4)]
    mates_z = [(g, 4 * lax.rem(z + k, 4) + y) for k in range(1, 4)]
    for target in mates + peers:
        pl.semaphore_signal(barrier, inc=1, device_id=target, device_id_type=MESH)

    map_mine[...] = jnp.zeros((8, NR), jnp.int32)
    loads[0].wait()
    map_mine[0:1, 0:NC] = cmap[...]
    tile = jnp.broadcast_to(map_mine[0:1, :], (8, NR))
    tile = pltpu.roll(tile, NC * lax.rem(s, 4), 1)
    at_row = lax.broadcasted_iota(jnp.int32, (8, NR), 0) == lax.div(s, 4)
    map_mine[...] = jnp.where(at_row, tile, 0)

    for load in loads[1:6]:
        load.wait()
    pl.semaphore_wait(barrier, len(mates) + len(peers))

    around = [
        (g, lax.rem(s + 1, N_SUB)),
        (g, lax.rem(s + N_SUB - 1, N_SUB)),
        (lax.rem(g + 1, N_GROUP), s),
        (lax.rem(g + N_GROUP - 1, N_GROUP), s),
    ]

    def send_zone(e, d, src, dst):
        remote(src, dst.at[d ^ 1], xs.at[e], xr.at[e, d ^ 1], around[d])
        if d == 3:
            started.append((dst, xs.at[e]))

    def ship(e, zones, values):
        tops = [
            jnp.maximum(jnp.max(jnp.abs(v), axis=0, keepdims=True), 2e-34) for v in values
        ]
        steps = [jnp.round(v * (32767.0 / t)) for v, t in zip(values, tops)]
        for d, value, top_value, codes in zip(zones, values, tops, steps):
            sent[e - 1, zone(d), :] = value
            step_mine[e - 1, d] = jnp.broadcast_to(top_value * (1.0 / 32767.0), (8, NR))
            coded[e - 1, zone(d), :] = codes.astype(jnp.int32).astype(jnp.int16)
        for d in zones:
            remote(
                step_mine.at[e - 1, d], step_all.at[e - 1, d ^ 1], qs.at[e - 1], qr.at[e - 1],
                around[d],
            )
            send_zone(e, d, coded.at[e - 1, zone(d)], got.at[e - 1])
            if d == 3:
                started.append((step_all.at[e - 1], qs.at[e - 1]))

    def steps_arrived(e):
        arrived(step_all.at[e - 1], qr.at[e - 1])

    def shipped(e, d):
        steps = got[e - 1, d].astype(jnp.int32).astype(F32)
        return fold(dot(perm[d], split(steps))) * step_all[e - 1, d, 0:1, :]

    def zone_arrived(e, d):
        zones = got0 if e == 0 else got.at[e - 1]
        arrived(zones.at[d], xr.at[e, d])

    def zone(d):
        return pl.ds(ZONE * d, ZONE)

    for d in range(4):
        send_zone(0, d, rhs.at[zone(d)], got0)
    map_sent = transfer(
        [(map_mine, map_all.at[k], mates[k - 1]) for k in range(1, N_SUB)],
        map_all.at[pl.ds(0, N_SUB - 1)], ms.at[0], mr.at[0],
    )

    lane = lax.broadcasted_iota(jnp.int32, (1, ZONE), 1)
    at = lax.broadcasted_iota(jnp.int32, (ZONE, ZONE), 0)
    for d in range(4):
        mine = jnp.where(lane < counts[0:1, d : d + 1], rows[0, d : d + 1, :] - ZONE * d, -1)
        theirs = rows[1, d : d + 1, :] - ZONE * (d ^ 1)
        place = jnp.where(at == mine, 1.0, 0.0)
        times = 1.0 + jnp.sum(place, axis=1, keepdims=True)
        mult[zone(d), :] = jnp.broadcast_to(times, (ZONE, NR))
        weight[zone(d), :] = jnp.broadcast_to(1.0 / times, (ZONE, NR))
        pick = jnp.where(at == theirs, 1.0, 0.0).astype(BF)
        pairs_d = dot(place.astype(BF), pick, ((1,), (1,)))
        perm[d] = pairs_d.astype(BF)
        shared = (pairs_d * (1.0 / times)).astype(BF)
        g_mine[d] = dot(basis[:, zone(d)], shared).astype(BF)
    g_sent = transfer(
        [(g_mine.at[d], g_all.at[d ^ 1], around[d]) for d in range(4)], g_all, gs.at[0], gr.at[0]
    )

    for zones in ((2, 3), (0, 1)):
        for d in zones:
            zone_arrived(0, d)
        whole = [rhs[zone(d), :].astype(F32) + dot(perm[d], got0[d]) for d in zones]
        halves = [split(weight[zone(d), :] * v) for d, v in zip(zones, whole)]
        for d, value, pair in zip(zones, whole, halves):
            r0[zone(d), :] = value
            xw[0, zone(d), :] = pair

    def coarse_send(k, local):
        cl_mine[k] = local
        cl_all[k, s] = local
        return transfer(
            [(cl_mine.at[k], cl_all.at[k, s], t) for t in mates],
            cl_all.at[k, pl.ds(0, N_SUB - 1)], cs.at[k], cr.at[k],
        )

    def coarse_setup():
        arrived(*map_sent)
        total = map_mine[...]
        for k in range(1, N_SUB):
            total = total + map_all[k]
        at_all = lax.broadcasted_iota(jnp.int32, (NL, NR), 0)
        for i in range(4):
            hot[:, NR * i : NR * (i + 1)] = jnp.where(
                at_all == total[i : i + 1, :], 1.0, 0.0
            ).astype(BF)
        picks = dot(cinv[...], hot[...]).T
        picks = jnp.concatenate([picks, picks], axis=1)
        half = lax.broadcasted_iota(jnp.int32, (NC_ALL, NR), 1) // OWN_ROWS
        picks = jnp.where(half == lax.rem(s, 2), picks, 0.0).astype(BF)
        e_mine[...] = picks.reshape(N_SUB, NC, NR)
        e_all[s] = e_mine[s]
        return transfer(
            [
                (e_mine.at[lax.rem(s + k, N_SUB)], e_all.at[s], mates[k - 1])
                for k in range(1, N_SUB)
            ],
            e_all.at[pl.ds(0, N_SUB - 1)], es.at[0], er.at[0],
        )

    def coarse_finish(e_sent):
        arrived(*e_sent)
        picks = jnp.concatenate([e_all[2 * i] + e_all[2 * i + 1] for i in range(N_SUB // 2)], axis=1)
        coarse[...] = dot(picks, hot[...]).astype(BF)

    def local_apply(matrix, blocks, d):
        return fold(dot(matrix[zone(d), :], blocks))

    def local_part(k, e):
        blocks = xw[k]
        for zones in ((0, 1), (2, 3)):
            ship(e, zones, [weight[zone(d), :] * local_apply(linv, blocks, d) for d in zones])

    def coarse_part(k, e, gathered):
        arrived(*gathered)
        terms = split(cl_all[k].reshape(NC_ALL, NR))
        values = fold(dot(coarse[...], terms))
        pk_mine[k] = values
        values_sent = transfer(
            [(pk_mine.at[k], pk_all.at[k, d ^ 1], around[d]) for d in range(4)],
            pk_all.at[k], ps.at[k], pr.at[k],
        )
        picked = split(values)
        for d in range(4):
            part = fold(dot(basis[:, zone(d)], picked, ((0,), (0,))))
            loc[zone(d), :] = sent[e - 1, zone(d), :] + weight[zone(d), :] * part
        return values_sent

    def finish_z(k, e, values_sent):
        arrived(*values_sent)
        for d in range(4):
            theirs = fold(dot(g_all[d], split(pk_all[k, d]), ((0,), (0,))))
            loc[zone(d), :] = loc[zone(d), :] + theirs
        steps_arrived(e)
        for zones in ((2, 3), (0, 1)):
            for d in zones:
                zone_arrived(e, d)
            whole = [split(loc[zone(d), :] + shipped(e, d)) for d in zones]
            for d, value in zip(zones, whole):
                xz[k, zone(d), :] = value

    def shares_setup():
        row = lax.broadcasted_iota(jnp.int32, (ZONE, ZONE), 0)
        column = lax.broadcasted_iota(jnp.int32, (ZONE, ZONE), 1)
        own = jnp.zeros((NC, NL), F32)
        for d in range(4):
            both = jnp.concatenate([weight[zone(d), :], weight[zone(d), :]], axis=1)
            scaled = dot(basis[:, zone(d)], jnp.where(row == column, both, 0.0).astype(BF)).astype(BF)
            own = own + dot(scaled, schur[zone(d), :])
            put_rows(d, dot(g_all[d], schur[zone(d), :]))
        put_rows(4, own)

    def put_rows(i, rows_f):
        hi = rows_f.astype(BF)
        gs_rows[pl.ds(2 * NC * i, NC), :] = hi
        gs_rows[pl.ds(2 * NC * i + NC, NC), :] = (rows_f - hi.astype(F32)).astype(BF)

    def operate(k, e, coarse_too):
        blocks = xz[k]
        if coarse_too:
            terms = fold(dot(gs_rows[...], blocks))
            terms = [
                terms[2 * NC * i : 2 * NC * i + NC] + terms[2 * NC * i + NC : 2 * NC * (i + 1)]
                for i in range(5)
            ]
            for d in range(4):
                ct_mine[k, d] = terms[d]
                remote(ct_mine.at[k, d], ct_all.at[k, d ^ 1], ts.at[k], tr.at[k], around[d])
            started.append((ct_all.at[k], ts.at[k]))
            own_share[...] = terms[4]
        for zones in ((0, 1), (2, 3)):
            ship(e, zones, [local_apply(schur, blocks, d) for d in zones])

    def coarse_shares(k, e):
        total = own_share[...]
        arrived(ct_all.at[k], tr.at[k])
        for d in range(4):
            total = total + ct_all[k, d]
        return coarse_send(k + 1, total)

    def finish_q(k, e):
        steps_arrived(e)
        for zones in ((2, 3), (0, 1)):
            for d in zones:
                zone_arrived(e, d)
            whole = [
                split(weight[zone(d), :] * (sent[e - 1, zone(d), :] + shipped(e, d))) for d in zones
            ]
            for d, value in zip(zones, whole):
                xw[k + 1, zone(d), :] = value

    def reduce_start(i):
        share = AR_ROWS[i] // N_GROUP

        def part(t):
            return pl.ds(pl.multiple_of(share * t, 8), share)

        ar_r1[i][g] = ar_in[i][part(g), :]
        return transfer(
            [(ar_in[i].at[part(t[0])], ar_r1[i].at[g], t) for t in peers],
            ar_r1[i].at[pl.ds(0, N_GROUP - 1)], as1.at[i], ar1.at[i],
        )

    def reduce_spread(i, step, total, targets, send_sem, recv_sem):
        ar_p[i][step] = total
        slot = (s, lax.rem(s, 4), lax.div(s, 4))[step]
        ar_r2[i][step, slot] = total
        return transfer(
            [(ar_p[i].at[step], ar_r2[i].at[step, slot], t) for t in targets],
            ar_r2[i].at[step, pl.ds(0, len(targets))], send_sem.at[i], recv_sem.at[i],
        )

    def reduce_sum(i, step, waits, count):
        arrived(*waits)
        total = ar_r2[i][step, 0]
        for k in range(1, count):
            total = total + ar_r2[i][step, k]
        return total

    def reduce_middle(i, waits):
        arrived(*waits)
        total = ar_r1[i][0]
        for k in range(1, N_GROUP):
            total = total + ar_r1[i][k]
        if i in (1, 2, 3):
            return reduce_spread(i, 0, total, mates, as2, ar2)
        return reduce_spread(i, 1, total, mates_y, as2, ar2)

    def reduce_more(i, waits):
        return reduce_spread(i, 2, reduce_sum(i, 1, waits, 4), mates_z, as4, ar4)

    def reduce_last(i, waits):
        share = AR_ROWS[i] // N_GROUP
        total = reduce_sum(i, 0, waits, N_SUB) if i in (1, 2, 3) else reduce_sum(i, 2, waits, 4)
        ar_q[i][...] = total
        mine = pl.ds(pl.multiple_of(share * g, 8), share)
        ar_out[i][mine, :] = total
        return transfer(
            [(ar_q[i], ar_out[i].at[mine], t) for t in peers],
            ar_out[i].at[pl.ds(0, share * (N_GROUP - 1))], as3.at[i], ar3.at[i],
        )

    def reduce_wait(waits):
        arrived(*waits)

    gathered = coarse_send(0, fold(dot(basis[...], xw[0])))
    e_sent = coarse_setup()
    load_l.wait()
    local_part(0, 1)
    arrived(*g_sent)
    load_s.wait()
    shares_setup()
    coarse_finish(e_sent)
    values_sent = coarse_part(0, 1, gathered)
    finish_z(0, 1, values_sent)

    operate(0, 2, True)
    gathered = coarse_shares(0, 2)
    ar_in[0][0:NR, :] = gram(xz[0], xw[0])
    finish_q(0, 2)
    local_part(1, 3)
    ar_in[0][NR:, :] = gram(xz[0], xw[1])
    ar_a = reduce_start(0)
    values_sent = coarse_part(1, 3, gathered)
    ar_a = reduce_middle(0, ar_a)
    finish_z(1, 3, values_sent)

    operate(1, 4, True)
    ar_a = reduce_more(0, ar_a)
    gathered = coarse_shares(1, 4)
    ar_in[1][0:NR, :] = gram(xz[1], xw[1])
    ar_a = reduce_last(0, ar_a)
    finish_q(1, 4)
    local_part(2, 5)
    ar_in[1][NR:, :] = gram(xz[1], xw[2])
    ar_b = reduce_start(1)
    values_sent = coarse_part(2, 5, gathered)
    reduce_wait(ar_a)
    mat[0] = sym(ar_out[0][NR:, :])
    invert_lead(top.at[0], mat.at[0])
    ar_b = reduce_middle(1, ar_b)
    finish_z(2, 5, values_sent)

    operate(2, 6, False)
    ar_in[2][...] = gram(xz[2], xw[2])
    ar_c = reduce_start(2)
    invert_steps(top.at[0], 0, 64)
    invert_next(top.at[0], bottom.at[0], mat.at[0])
    ar_b = reduce_last(1, ar_b)
    finish_q(2, 6)
    ar_in[3][...] = gram(xz[2], xw[3])
    ar_d = reduce_start(3)
    ar_c = reduce_middle(2, ar_c)
    invert_steps(bottom.at[0], 0, 64)
    inv1 = invert_end(top.at[0], bottom.at[0])
    m0 = ar_out[0][0:NR, :]
    t0 = small(inv1, m0)
    reduce_wait(ar_b)
    m2 = sym(ar_out[1][0:NR, :])
    m3 = sym(ar_out[1][NR:, :])
    t2 = small(inv1, m2)
    mat[1] = sym(m3 - small(m2, t2))
    invert_lead(top.at[1], mat.at[1])
    ar_d = reduce_middle(3, ar_d)
    invert_steps(top.at[1], 0, 64)
    invert_next(top.at[1], bottom.at[1], mat.at[1])
    ar_c = reduce_last(2, ar_c)
    invert_steps(bottom.at[1], 0, 32)
    ar_d = reduce_last(3, ar_d)
    invert_steps(bottom.at[1], 32, 64)
    inv2 = invert_end(top.at[1], bottom.at[1])
    t3 = small(inv1, m3)
    h1 = mat[0] - small(m2, t0)
    reduce_wait(ar_c)
    m4 = sym(ar_out[2][...])
    s23 = m4 - small(m2, t3)
    y = small(inv2, s23)
    u1 = small(inv2, h1)
    h2 = m2 - small(m3, t0) - small_t(s23, u1)
    part = small(m3, t3) + small_t(s23, y)
    a0 = t0 - small(t2, u1)
    d0 = small(t2, y) - t3
    reduce_wait(ar_d)
    mat[2] = sym(ar_out[3][...] - part)
    invert_lead(top.at[2], mat.at[2])
    invert_steps(top.at[2], 0, 64)
    invert_next(top.at[2], bottom.at[2], mat.at[2])
    cross = top[2, :, HALF:]
    above = small(top[2, :, :HALF], h2[:HALF])
    below = h2[HALF:] - small_t(cross, h2[:HALF])
    invert_steps(bottom.at[2], 0, 64)
    below = small(bottom[2, :, :HALF], below)
    c2 = jnp.concatenate([above - small(cross, below), below], axis=0)
    c1 = u1 - small(y, c2)
    c0 = a0 + small(d0, c2)
    x_out[...] = combine(xz[0], c0) + combine(xz[1], c1) + combine(xz[2], c2)
    r_out[...] = r0[...] - mult[...] * (combine(xw[1], c0) + combine(xw[2], c1) + combine(xw[3], c2))
    for span, sem in started:
        arrived(span, sem)


def shards(
    schur, local_inverse, rhs_parts, basis, coarse_map, coarse_inverse, shared_rows, shared_counts
):
    vmem = pl.BlockSpec(memory_space=pltpu.VMEM)
    in_hbm = pl.BlockSpec(memory_space=pltpu.HBM)
    dma = pltpu.SemaphoreType.DMA
    ar_shapes = [r // N_GROUP for r in AR_ROWS]
    scratch = [
        pltpu.VMEM((NL, NL), BF),
        pltpu.VMEM((NL, NL), BF),
        pltpu.VMEM((NL, NR), BF),
        pltpu.VMEM((NC, NL), BF),
        pltpu.VMEM((1, NC), jnp.int32),
        pltpu.VMEM((OWN_ROWS, NL), BF),
        pltpu.VMEM((2, 4, ZONE), jnp.int32),
        pltpu.VMEM((1, 4), jnp.int32),
        pltpu.VMEM((4, ZONE, ZONE), BF),
        pltpu.VMEM((NL, NR), F32),
        pltpu.VMEM((NL, NR), F32),
        pltpu.VMEM((6, NL, NR), F32),
        pltpu.VMEM((6, NL, NR), jnp.int16),
        pltpu.VMEM((6, 4, 8, NR), F32),
        pltpu.VMEM((6, 4, 8, NR), F32),
        pltpu.VMEM((4, ZONE, NR), BF),
        pltpu.VMEM((6, 4, ZONE, NR), jnp.int16),
        pltpu.VMEM((NL, NR), F32),
        pltpu.VMEM((4, NL, 2 * NR), BF),
        pltpu.VMEM((3, NL, 2 * NR), BF),
        pltpu.VMEM((NL, NR), F32),
        pltpu.VMEM((3, NC, NR), F32),
        pltpu.VMEM((3, N_SUB, NC, NR), F32),
        pltpu.VMEM((8, NR), jnp.int32),
        pltpu.VMEM((N_SUB, 8, NR), jnp.int32),
        pltpu.VMEM((NL, NC_ALL), BF),
        pltpu.VMEM((N_SUB, NC, NR), BF),
        pltpu.VMEM((N_SUB, NC, NR), BF),
        pltpu.VMEM((NC, NC_ALL), BF),
        pltpu.VMEM((3, NR, NR), F32),
        pltpu.VMEM((3, HALF, NR), F32),
        pltpu.VMEM((3, HALF, NR), F32),
        pltpu.VMEM((4, NC, ZONE), BF),
        pltpu.VMEM((4, NC, ZONE), BF),
        pltpu.VMEM((2, 4, NC, NR), F32),
        pltpu.VMEM((2, 4, NC, NR), F32),
        pltpu.VMEM((10 * NC, NL), BF),
        pltpu.VMEM((NC, NR), F32),
        pltpu.VMEM((3, NC, NR), F32),
        pltpu.VMEM((3, 4, NC, NR), F32),
        [pltpu.VMEM((r, NR), F32) for r in AR_ROWS],
        [pltpu.VMEM((N_GROUP, r, NR), F32) for r in ar_shapes],
        [pltpu.VMEM((3, r, NR), F32) for r in ar_shapes],
        [pltpu.VMEM((3, N_SUB, r, NR), F32) for r in ar_shapes],
        [pltpu.VMEM((r, NR), F32) for r in ar_shapes],
        [pltpu.VMEM((r, NR), F32) for r in AR_ROWS],
        dma((8,)),
        dma((7,)),
        dma((7, 4)),
        dma((3,)),
        dma((3,)),
        dma((1,)),
        dma((1,)),
        dma((1,)),
        dma((1,)),
        dma((4,)),
        dma((4,)),
        dma((4,)),
        dma((4,)),
        dma((4,)),
        dma((4,)),
        dma((4,)),
        dma((4,)),
        dma((1,)),
        dma((1,)),
        dma((2,)),
        dma((2,)),
        dma((3,)),
        dma((3,)),
        dma((6,)),
        dma((6,)),
    ]
    out = jax.ShapeDtypeStruct((NL, NR), F32)
    x, r = pl.pallas_call(
        kernel,
        out_shape=(out, out),
        in_specs=[in_hbm] * 8,
        out_specs=(vmem, vmem),
        scratch_shapes=scratch,
        compiler_params=pltpu.CompilerParams(
            collective_id=0, has_side_effects=True, vmem_limit_bytes=40 * 1024 * 1024
        ),
        name="block_cg",
    )(
        *[
            pltpu.with_memory_space_constraint(a, pltpu.HBM)
            for a in (
                schur[0, 0], local_inverse[0, 0], rhs_parts[0, 0], basis[0, 0], coarse_map[0],
                coarse_inverse[0], shared_rows[0, 0], shared_counts[0],
            )
        ]
    )
    return x[None, None], r[None, None]


def solution(mesh):
    placed = (
        P("group", "sub", None, None),
        P("group", "sub", None, None),
        P("group", "sub", None, None),
        P("group", "sub", None, None),
        P("group", "sub", None),
        P("group", "sub", None),
        P("group", "sub", None, None, None),
        P("group", "sub", None),
    )
    return jax.shard_map(
        shards,
        mesh=mesh,
        in_specs=placed,
        out_specs=(P("group", "sub", None, None), P("group", "sub", None, None)),
        check_vma=False,
    )
```
